128 devices in a mesh: row: 16 (over x, y_hi, core), col: 8 (over z, y_lo).
Axes of the slice: x: 4, y: 4 (y_hi: 2, y_lo: 2; y = y_hi * 2 + y_lo), z: 4, core: 2. Of those that a mesh axis runs over, the one named last changes fastest.
Arguments:
- left_pairs: float32 [20480, 1536], P('row', 'col'), may hold values from -6 to 6
- right_pairs: float32 [1536, 20480], P('row', 'col'), may hold values from -0.15625 to 0.15625
- pair_weight: float32 [1536], P('row'), may hold values from 0.3 to 3
- screen: float32 [20480], replicated, may hold values from 6 to 12
- panel_index: int32 [2], replicated, may hold values from 0 to 79, as said below
Outputs:
- dielectric: float32 [20480, 20480], P('row', 'col')
The draws below stay inside these ranges and needn't reach their ends.
Inputs may be any that keep to these rules, and one draw needn't show every extreme that they name: `panel_index`: two different block indices; one of them, at either section, is the last block 79, the other lies in 0 to 78.
All inputs are finite; a program needn't handle non-finite values.
Results may differ from the reference program's by a relative error of at most 0.0001.
Values sent between devices are 32-bit elements; how exact they have to be, the bound alone decides.
A program may use at most 128 MiB of HBM per device.

```python
import math
import jax
import jax.numpy as jnp
from jax import lax

NPW = 20480
PAIRS = 1536
PANEL = 256
SECTIONS = 2
NS_STEPS = 3


def draw_panel_index(key, part):
    block_count = NPW // PANEL
    first_key, second_key = jax.random.split(jax.random.fold_in(key, 7))
    other_block = jax.random.randint(first_key, (), 0, block_count - 1)
    last_first = jax.random.randint(second_key, (), 0, 2)
    last_block = jnp.int32(block_count - 1)
    leading = jnp.where(last_first == 1, last_block, other_block)
    trailing = jnp.where(last_first == 1, other_block, last_block)
    return jnp.stack([leading, trailing]).astype(jnp.int32)


def shard_levels(rng, shape, shards, least, largest):
    def one(axis_at, parts):
        heights = jax.random.uniform(jax.random.fold_in(jax.random.fold_in(rng, 6), axis_at), (parts,), jnp.float32, least / len(shards), largest / len(shards))
        return jnp.repeat(jnp.exp(heights), shape[axis_at] // parts).reshape((-1,) + (1,) * (len(shape) - axis_at - 1))

    loudness = one(*shards[0])
    for cut in shards[1:]:
        loudness = loudness * one(*cut)
    return loudness


def scatter_about(stream_key, dims, spread, bound, shards=(), held_as=jnp.bfloat16):
    result = jax.random.normal(stream_key, dims, jnp.float32) * spread
    if len(shards) > 0:
        result = shard_levels(stream_key, dims, shards, -0.22, 0.18) * result
    return jnp.clip(result, min=-bound, max=bound).astype(held_as)


def setup_inputs(seed: int = 0) -> dict:
    splits = jax.random.split(jax.random.key(seed), 6)
    left_pairs = scatter_about(splits[0], (NPW, PAIRS), 1.0, 6.0, ((0, 16), (1, 8)), jnp.float32)
    right_pairs = scatter_about(splits[1], (PAIRS, NPW), PAIRS ** -0.5, 0.15625, ((0, 16), (1, 8)), jnp.float32)
    pair_weight = jnp.clip(jnp.exp(math.log(3.0) - 2.3025851 * jax.random.uniform(splits[2], (PAIRS,), jnp.float32) ** shard_levels(splits[2], (PAIRS,), ((0, 16),), -0.2, 0.2)), 0.3, 3.0)
    screen = jnp.clip(jax.random.uniform(splits[3], (NPW,), jnp.float32, 6.0, 12.0), 6.0, 12.0)
    panel_index = draw_panel_index(jax.random.fold_in(splits[5], 71), 0)
    return {"left_pairs": left_pairs, "right_pairs": right_pairs, "pair_weight": pair_weight, "screen": screen, "panel_index": panel_index}


COUPLING = 0.08


def newton_inverse(matrix_in):
    eye = jnp.eye(matrix_in.shape[0], dtype=jnp.float32)
    approx = eye / jnp.diagonal(matrix_in)[None, :]
    for section in range(NS_STEPS):
        product = jnp.dot(matrix_in, approx, precision=lax.Precision.HIGHEST, preferred_element_type=jnp.float32)
        approx = jnp.dot(approx, 2.0 * eye - product, precision=lax.Precision.HIGHEST, preferred_element_type=jnp.float32)
    return approx


def reference(left_pairs, right_pairs, pair_weight, screen, panel_index):
    weighted = right_pairs * pair_weight[:, None]
    polar = jnp.dot(left_pairs, weighted, precision=lax.Precision.HIGHEST, preferred_element_type=jnp.float32)
    positions = jnp.arange(NPW, dtype=jnp.int32)
    dielectric = COUPLING * polar
    dielectric = dielectric.at[positions, positions].add(screen)
    finished = jnp.zeros((NPW,), dtype=bool)
    for section in range(SECTIONS):
        anchor = (panel_index[section] * PANEL).astype(jnp.int32)
        inside = (positions >= anchor) & (positions < anchor + PANEL)
        remain = jnp.logical_not(finished | inside)
        column = lax.dynamic_slice_in_dim(dielectric, anchor, PANEL, 1)
        row_panel = lax.dynamic_slice_in_dim(dielectric, anchor, PANEL, 0)
        pivot_block = lax.dynamic_slice_in_dim(row_panel, anchor, PANEL, 1)
        inverse = newton_inverse(pivot_block)
        lower_part = jnp.dot(column, inverse, precision=lax.Precision.HIGHEST, preferred_element_type=jnp.float32)
        lower_part = lower_part * remain[:, None].astype(jnp.float32)
        masked_rows = row_panel * remain[None, :].astype(jnp.float32)
        dielectric = dielectric - jnp.dot(lower_part, masked_rows, precision=lax.Precision.HIGHEST, preferred_element_type=jnp.float32)
        patched = jnp.where(remain[:, None], lower_part, column)
        dielectric = lax.dynamic_update_slice_in_dim(dielectric, patched, anchor, 1)
        finished = finished | inside
    return dielectric
```

```python
import jax
import jax.numpy as jnp
from jax import lax
from jax.experimental import pallas as pl
from jax.experimental.pallas import tpu as pltpu
from jax.sharding import PartitionSpec as P

PANEL = 256
SECTIONS = 2
NS_STEPS = 3

COUPLING = 0.08

MESH = pl.DeviceIdType.MESH
F32 = jnp.float32


def remote(src, dst, send_sem, recv_sem, target):
    return pltpu.make_async_remote_copy(
        src_ref=src,
        dst_ref=dst,
        send_sem=send_sem,
        recv_sem=recv_sem,
        device_id=target,
        device_id_type=MESH,
    )


class Ring:
    def __init__(self, ref, me, ahead, behind, send_sems, recv_sems, base):
        self.ref, self.me = ref, me
        self.ahead, self.behind = ahead, behind
        self.send_sems, self.recv_sems, self.base = send_sems, recv_sems, base
        self.sent = []

    def pos(self, step):
        return lax.rem(self.me + 4 + step, 4)

    def send(self, src, pos, half, key, target):
        copy = remote(
            src,
            self.ref(pos, half),
            self.send_sems.at[self.base + key],
            self.recv_sems.at[self.base + key],
            target,
        )
        copy.start()
        self.sent.append(copy)

    def arrived(self, pos, half, key):
        ref = self.ref(pos, half)
        remote(
            ref,
            ref,
            self.send_sems.at[self.base + key],
            self.recv_sems.at[self.base + key],
            self.ahead,
        ).wait_recv()

    def start(self, half_at, source=None):
        source = source or (lambda half: self.ref(self.me, half))
        first, second = (0, 1) if half_at == 0 else (1, 0)
        self.send(source(first), self.me, first, first, self.ahead)
        self.send(source(second), self.me, second, 2 + second, self.behind)

    def forward(self):
        self.arrived(self.pos(-1), 0, 0)
        self.send(self.ref(self.pos(-1), 0), self.pos(-1), 0, 4, self.ahead)
        self.arrived(self.pos(1), 1, 3)
        self.send(self.ref(self.pos(1), 1), self.pos(1), 1, 5, self.behind)

    def finish_near(self):
        self.arrived(self.pos(-1), 1, 1)
        self.arrived(self.pos(1), 0, 2)

    def finish_far(self):
        self.arrived(self.pos(2), 0, 4)
        self.arrived(self.pos(2), 1, 5)

    def drain(self):
        for copy in self.sent:
            copy.wait_send()


def gather_kernel(
    left_ref,
    right_ref,
    lp_ref,
    wp_ref,
    l_ref,
    w_ref,
    p_ref,
    lp_in,
    wp_in,
    piece,
    send_sems,
    recv_sems,
    lps_sems,
    lpr_sems,
    wps_sems,
    wpr_sems,
    local_sems,
):
    r = lax.axis_index("row")
    c = lax.axis_index("col")
    core = lax.rem(r, 2)
    yh = lax.rem(r // 2, 2)
    x = r // 4
    yl = lax.rem(c, 2)
    z = c // 2
    y = yh * 2 + yl

    def at(x=x, y=y, z=z, core=core):
        return {"row": (x * 2 + y // 2) * 2 + core, "col": z * 2 + lax.rem(y, 2)}

    x_up, x_down = at(x=lax.rem(x + 1, 4)), at(x=lax.rem(x + 3, 4))
    z_up, z_down = at(z=lax.rem(z + 1, 4)), at(z=lax.rem(z + 3, 4))
    y_up, y_down = at(y=lax.rem(y + 1, 4)), at(y=lax.rem(y + 3, 4))
    far = at(y=lax.rem(y + 2, 4))
    near = at(y=yh * 2 + 1 - yl)
    other = at(core=1 - core)

    own_l = pltpu.make_async_copy(left_ref, l_ref.at[c], local_sems.at[0])
    own_w = pltpu.make_async_copy(right_ref, w_ref.at[r], local_sems.at[1])
    own_l.start()
    own_w.start()

    barrier = pltpu.get_barrier_semaphore()

    def greet_row(k, carry):
        pl.semaphore_signal(
            barrier, 1, device_id={"row": lax.rem(r + k, 16), "col": c}, device_id_type=MESH
        )
        return carry

    def greet_col(k, carry):
        pl.semaphore_signal(
            barrier, 1, device_id={"row": r, "col": lax.rem(c + k, 8)}, device_id_type=MESH
        )
        return carry

    lax.fori_loop(1, 16, greet_row, 0)
    lax.fori_loop(1, 8, greet_col, 0)
    across = at(y=lax.rem(y + 3 + 2 * yl, 4))
    pl.semaphore_signal(barrier, 1, device_id=across, device_id_type=MESH)
    pl.semaphore_wait(barrier, 23)

    def lp_copy(k):
        to = lax.rem(r + k, 16)
        return remote(
            lp_ref.at[to], lp_in.at[r], lps_sems.at[k], lpr_sems.at[k], {"row": to, "col": c}
        )

    def wp_copy(k):
        to = lax.rem(c + k, 8)
        return remote(
            wp_ref.at[to], wp_in.at[c], wps_sems.at[k], wpr_sems.at[k], {"row": r, "col": to}
        )

    for k in range(1, 16):
        lp_copy(k).start()
    for k in range(1, 8):
        wp_copy(k).start()

    def w_place(yh_of):
        def place(pos, half):
            return w_ref.at[(pos * 2 + yh_of) * 2 + core, pl.ds(half * 48, 48), :]

        return place

    def l_place(yl_of):
        def place(pos, half):
            return l_ref.at[pos * 2 + yl_of, pl.ds(half * 96, 96), :]

        return place

    w_rings = [
        Ring(w_place(yh), x, x_up, x_down, send_sems, recv_sems, 0),
        Ring(w_place(1 - yh), x, x_up, x_down, send_sems, recv_sems, 6),
    ]
    l_rings = [
        Ring(l_place(yl), z, z_up, z_down, send_sems, recv_sems, 12),
        Ring(l_place(1 - yl), z, z_up, z_down, send_sems, recv_sems, 18),
    ]

    def w_own(half):
        return right_ref.at[pl.ds(half * 48, 48), :]

    def l_own(half):
        return left_ref.at[pl.ds(half * 96, 96), :]

    swaps = []

    def swap(src, dst, key, target):
        copy = remote(src, dst, send_sems.at[key], recv_sems.at[key], target)
        copy.start()
        swaps.append(copy)

    for half in range(2):
        w_rings[0].start(half, w_own)
        l_rings[0].start(half, l_own)
        swap(w_own(half), w_place(yh)(x, half), 24 + half, far)
        swap(l_own(half), l_place(yl)(z, half), 26 + half, near)

    def to_other(pos, yh_of, key):
        slot = w_ref.at[(pos * 2 + yh_of) * 2 + core]
        swap(slot, slot, key, other)

    def swapped(place, pos, half, key):
        ref = place(pos, half)
        remote(ref, ref, send_sems.at[key], recv_sems.at[key], other).wait_recv()

    own_w.wait()
    own_l.wait()
    to_other(x, yh, 28)
    total_l = lp_ref[r]
    for k in range(1, 16):
        lp_copy(k).wait_recv()
    for k in range(1, 16):
        total_l = total_l + lp_in[lax.rem(r + 16 - k, 16)]
    total_w = wp_ref[c]
    for k in range(1, 8):
        wp_copy(k).wait_recv()
    for k in range(1, 8):
        total_w = total_w + wp_in[lax.rem(c + 8 - k, 8)]
    piece[pl.ds(0, 24), :] = total_l
    piece[pl.ds(24, 24), :] = total_w
    own_p = pltpu.make_async_copy(piece, p_ref.at[core, y, x, z], local_sems.at[2])
    own_p.start()

    pz = Ring(
        lambda pos, half: p_ref.at[core, y, x, pos, pl.ds(half * 24, 24), :],
        z, z_up, z_down, send_sems, recv_sems, 36,
    )
    px = Ring(
        lambda pos, half: p_ref.at[core, y, pos, pl.ds(half * 2, 2)],
        x, x_up, x_down, send_sems, recv_sems, 42,
    )
    py = Ring(
        lambda pos, half: p_ref.at[core, pos, pl.ds(half * 2, 2)],
        y, y_up, y_down, send_sems, recv_sems, 48,
    )
    for half in range(2):
        pz.start(half, lambda h: piece.at[pl.ds(h * 24, 24), :])
    pz.forward()
    own_p.wait()
    pz.finish_near()
    pz.finish_far()
    for half in range(2):
        px.start(half)
    px.forward()
    px.finish_near()
    px.finish_far()
    for half in range(2):
        py.start(half)

    w_rings[0].forward()
    l_rings[0].forward()
    for half in range(2):
        swapped(w_place(1 - yh), x, half, 24 + half)
        swapped(l_place(1 - yl), z, half, 26 + half)
    for half in range(2):
        w_rings[1].start(half)
        l_rings[1].start(half)
    py.forward()
    to_other(x, 1 - yh, 29)
    w_rings[0].finish_near()
    to_other(w_rings[0].pos(-1), yh, 30)
    to_other(w_rings[0].pos(1), yh, 31)
    py.finish_near()
    py.finish_far()
    swap(p_ref.at[core], p_ref.at[core], 54, other)
    w_rings[0].finish_far()
    to_other(w_rings[0].pos(2), yh, 32)
    w_rings[1].forward()
    l_rings[1].forward()
    w_rings[1].finish_near()
    to_other(w_rings[0].pos(-1), 1 - yh, 33)
    to_other(w_rings[0].pos(1), 1 - yh, 34)
    w_rings[1].finish_far()
    to_other(w_rings[0].pos(2), 1 - yh, 35)
    for ring in l_rings:
        ring.finish_near()
        ring.finish_far()

    def from_other(pos, yh_of, key):
        slot = w_ref.at[(pos * 2 + yh_of) * 2 + 1 - core]
        remote(slot, slot, send_sems.at[key], recv_sems.at[key], other).wait_recv()

    ring = w_rings[0]
    from_other(x, yh, 28)
    from_other(x, 1 - yh, 29)
    from_other(ring.pos(-1), yh, 30)
    from_other(ring.pos(1), yh, 31)
    from_other(ring.pos(2), yh, 32)
    from_other(ring.pos(-1), 1 - yh, 33)
    from_other(ring.pos(1), 1 - yh, 34)
    from_other(ring.pos(2), 1 - yh, 35)
    panels = p_ref.at[1 - core]
    remote(panels, panels, send_sems.at[54], recv_sems.at[54], other).wait_recv()

    for k in range(1, 16):
        lp_copy(k).wait_send()
    for k in range(1, 8):
        wp_copy(k).wait_send()
    for ring in w_rings + l_rings + [pz, px, py]:
        ring.drain()
    for copy in swaps:
        copy.wait_send()


def gather(left_t, right, lp, wp):
    any_spec = pl.BlockSpec(memory_space=pl.ANY)
    vmem_spec = pl.BlockSpec(memory_space=pltpu.VMEM)
    dma = pltpu.SemaphoreType.DMA
    return pl.pallas_call(
        gather_kernel,
        out_shape=(
            jax.ShapeDtypeStruct((8, 192, 1280), F32),
            jax.ShapeDtypeStruct((16, 96, 2560), F32),
            jax.ShapeDtypeStruct((2, 4, 4, 4, 48, 256), F32),
        ),
        in_specs=[any_spec, any_spec, vmem_spec, vmem_spec],
        out_specs=(any_spec, any_spec, any_spec),
        scratch_shapes=[
            pltpu.VMEM((16, 24, 256), F32),
            pltpu.VMEM((8, 24, 256), F32),
            pltpu.VMEM((48, 256), F32),
            dma((55,)),
            dma((55,)),
            dma((16,)),
            dma((16,)),
            dma((8,)),
            dma((8,)),
            dma((3,)),
        ],
        compiler_params=pltpu.CompilerParams(collective_id=0, has_side_effects=True),
        name="gather",
    )(left_t, right, lp, wp)


def dot(a, b, precision=lax.Precision.HIGH, dims=((1,), (0,))):
    return lax.dot_general(
        a, b, (dims, ((), ())), precision=precision, preferred_element_type=F32
    )


def newton_inverse(matrix_in):
    eye = jnp.eye(matrix_in.shape[0], dtype=F32)
    diagonal = jnp.sum(matrix_in * eye, axis=0)
    approx = eye / diagonal[None, :]
    for _ in range(NS_STEPS):
        product = dot(matrix_in, approx)
        approx = dot(approx, 2.0 * eye - product)
    return approx


def shards(left_pairs, right_pairs, pair_weight, screen, panel_index):
    left_t = left_pairs.T
    weighted = right_pairs * pair_weight[:, None]
    rows_here = left_pairs.shape[0]
    cols_here = weighted.shape[1]
    row_start = lax.axis_index("row") * rows_here
    col_start = lax.axis_index("col") * cols_here

    lp, wp = [], []
    for section in range(SECTIONS):
        anchor = panel_index[section] * PANEL
        at_row = anchor - row_start
        at_col = anchor - col_start
        here_row = (at_row >= 0) & (at_row < rows_here)
        here_col = (at_col >= 0) & (at_col < cols_here)
        part = lax.dynamic_slice_in_dim(left_t, jnp.clip(at_row, 0, rows_here - PANEL), PANEL, 1)
        lp.append(jnp.where(here_row, part, 0.0).reshape(8, 24, PANEL))
        part = lax.dynamic_slice_in_dim(weighted, jnp.clip(at_col, 0, cols_here - PANEL), PANEL, 1)
        wp.append(jnp.where(here_col, part, 0.0).reshape(4, 24, PANEL))
    lp = jnp.stack(lp, axis=1).reshape(16, 24, PANEL)
    wp = jnp.stack(wp, axis=1).reshape(8, 24, PANEL)

    l_all, w_all, panels = gather(left_t, weighted, lp, wp)
    lt = l_all.reshape(1536, rows_here)
    w = w_all.reshape(1536, cols_here)
    panels = panels.reshape(2, 2, 2, 4, 4, 2, 24, PANEL)
    lk_t = panels[:, :, :, :, :, 0].transpose(4, 2, 3, 1, 5, 0, 6).reshape(1536, 2 * PANEL)
    wk = panels[:, :, :, :, :, 1].transpose(3, 1, 0, 4, 5, 2, 6).reshape(1536, 2 * PANEL)

    glob_rows = row_start + jnp.arange(rows_here, dtype=jnp.int32)
    glob_cols = col_start + jnp.arange(cols_here, dtype=jnp.int32)
    first, second = panel_index[0] * PANEL, panel_index[1] * PANEL

    def inside(positions, anchor):
        return (positions >= anchor) & (positions < anchor + PANEL)

    mask1 = jnp.logical_not(inside(glob_rows, first))
    mask2 = mask1 & jnp.logical_not(inside(glob_rows, second))
    eye = jnp.eye(PANEL, dtype=F32)
    screen1 = lax.dynamic_slice_in_dim(screen, first, PANEL, 0)
    screen2 = lax.dynamic_slice_in_dim(screen, second, PANEL, 0)

    x = COUPLING * dot(lk_t, wk, dims=((0,), (0,)))
    x11, x12 = x[:PANEL, :PANEL], x[:PANEL, PANEL:]
    x21, x22 = x[PANEL:, :PANEL], x[PANEL:, PANEL:]
    inv1 = newton_inverse(x11 + eye * screen1[None, :])
    b1 = dot(x21, inv1)
    inv2 = newton_inverse(x22 - dot(b1, x12) + eye * screen2[None, :])
    cols = COUPLING * dot(lt, wk, dims=((0,), (0,)))
    low1 = jnp.where(mask1[:, None], dot(cols[:, :PANEL], inv1), 0.0)
    low2 = jnp.where(mask2[:, None], dot(cols[:, PANEL:] - dot(low1, x12), inv2), 0.0)
    e = jnp.concatenate([low1 - dot(low2, b1), low2], axis=1)
    l_eff = lt - dot(lk_t, e, dims=((1,), (1,)))
    out = COUPLING * dot(l_eff, w, dims=((0,), (0,)))
    screen_rows = lax.dynamic_slice_in_dim(screen, row_start, rows_here, 0)
    out = out + jnp.where(glob_rows[:, None] == glob_cols[None, :], screen_rows[:, None], 0.0)
    for anchor, mask, low in ((first, mask1, low1), (second, mask2, low2)):
        at_col = anchor - col_start
        here = (at_col >= 0) & (at_col < cols_here)
        local = jnp.clip(at_col, 0, cols_here - PANEL)
        old = lax.dynamic_slice_in_dim(out, local, PANEL, 1)
        new = jnp.where(here & mask[:, None], low, old)
        out = lax.dynamic_update_slice_in_dim(out, new, local, 1)
    return out


def solution(mesh):
    return jax.shard_map(
        shards,
        mesh=mesh,
        in_specs=(P("row", "col"), P("row", "col"), P("row"), P(), P()),
        out_specs=P("row", "col"),
        check_vma=False,
    )
```

```python
import jax
import jax.numpy as jnp
from jax import lax
from jax.experimental import pallas as pl
from jax.experimental.pallas import tpu as pltpu
from jax.sharding import PartitionSpec as P

PANEL = 256
SECTIONS = 2
NS_STEPS = 3

COUPLING = 0.08

MESH = pl.DeviceIdType.MESH
F32 = jnp.float32
BF = jnp.bfloat16


def remote(src, dst, send_sem, recv_sem, target):
    return pltpu.make_async_remote_copy(
        src_ref=src,
        dst_ref=dst,
        send_sem=send_sem,
        recv_sem=recv_sem,
        device_id=target,
        device_id_type=MESH,
    )


class Ring:
    def __init__(self, ref, me, ahead, behind, send_sems, recv_sems, base):
        self.ref, self.me = ref, me
        self.ahead, self.behind = ahead, behind
        self.send_sems, self.recv_sems, self.base = send_sems, recv_sems, base
        self.sent = []

    def pos(self, step):
        return lax.rem(self.me + 4 + step, 4)

    def send(self, src, pos, half, key, target):
        copy = remote(
            src,
            self.ref(pos, half),
            self.send_sems.at[self.base + key],
            self.recv_sems.at[self.base + key],
            target,
        )
        copy.start()
        self.sent.append(copy)

    def arrived(self, pos, half, key):
        ref = self.ref(pos, half)
        remote(
            ref,
            ref,
            self.send_sems.at[self.base + key],
            self.recv_sems.at[self.base + key],
            self.ahead,
        ).wait_recv()

    def start(self, half_at, source=None):
        source = source or (lambda half: self.ref(self.me, half))
        first, second = (0, 1) if half_at == 0 else (1, 0)
        self.send(source(first), self.me, first, first, self.ahead)
        self.send(source(second), self.me, second, 2 + second, self.behind)

    def forward(self):
        self.arrived(self.pos(-1), 0, 0)
        self.send(self.ref(self.pos(-1), 0), self.pos(-1), 0, 4, self.ahead)
        self.arrived(self.pos(1), 1, 3)
        self.send(self.ref(self.pos(1), 1), self.pos(1), 1, 5, self.behind)

    def finish_near(self):
        self.arrived(self.pos(-1), 1, 1)
        self.arrived(self.pos(1), 0, 2)

    def finish_far(self):
        self.arrived(self.pos(2), 0, 4)
        self.arrived(self.pos(2), 1, 5)

    def drain(self):
        for copy in self.sent:
            copy.wait_send()


def gather_kernel(
    left_ref,
    right_ref,
    lp_ref,
    wp_ref,
    l_ref,
    w_ref,
    p_ref,
    lp_in,
    wp_in,
    piece,
    send_sems,
    recv_sems,
    lps_sems,
    lpr_sems,
    wps_sems,
    wpr_sems,
    local_sems,
    own_left,
    own_right,
):
    r = lax.axis_index("row")
    c = lax.axis_index("col")
    core = lax.rem(r, 2)
    yh = lax.rem(r // 2, 2)
    x = r // 4
    yl = lax.rem(c, 2)
    z = c // 2
    y = yh * 2 + yl

    def at(x=x, y=y, z=z, core=core):
        return {"row": (x * 2 + y // 2) * 2 + core, "col": z * 2 + lax.rem(y, 2)}

    x_up, x_down = at(x=lax.rem(x + 1, 4)), at(x=lax.rem(x + 3, 4))
    z_up, z_down = at(z=lax.rem(z + 1, 4)), at(z=lax.rem(z + 3, 4))
    y_up, y_down = at(y=lax.rem(y + 1, 4)), at(y=lax.rem(y + 3, 4))
    far = at(y=lax.rem(y + 2, 4))
    near = at(y=yh * 2 + 1 - yl)
    other = at(core=1 - core)

    own_l = pltpu.make_async_copy(left_ref, own_left, local_sems.at[0])
    own_w = pltpu.make_async_copy(right_ref, own_right, local_sems.at[1])
    own_l.start()
    own_w.start()
    put_l = pltpu.make_async_copy(own_left, l_ref.at[c], local_sems.at[3])
    put_w = pltpu.make_async_copy(own_right, w_ref.at[r], local_sems.at[4])

    barrier = pltpu.get_barrier_semaphore()

    def greet_row(k, carry):
        pl.semaphore_signal(
            barrier, 1, device_id={"row": lax.rem(r + k, 16), "col": c}, device_id_type=MESH
        )
        return carry

    def greet_col(k, carry):
        pl.semaphore_signal(
            barrier, 1, device_id={"row": r, "col": lax.rem(c + k, 8)}, device_id_type=MESH
        )
        return carry

    lax.fori_loop(1, 16, greet_row, 0)
    lax.fori_loop(1, 8, greet_col, 0)
    across = at(y=lax.rem(y + 3 + 2 * yl, 4))
    pl.semaphore_signal(barrier, 1, device_id=across, device_id_type=MESH)
    pl.semaphore_wait(barrier, 23)

    def lp_copy(k):
        to = lax.rem(r + k, 16)
        return remote(
            lp_ref.at[to], lp_in.at[r], lps_sems.at[k], lpr_sems.at[k], {"row": to, "col": c}
        )

    def wp_copy(k):
        to = lax.rem(c + k, 8)
        return remote(
            wp_ref.at[to], wp_in.at[c], wps_sems.at[k], wpr_sems.at[k], {"row": r, "col": to}
        )

    for k in range(1, 16):
        lp_copy(k).start()
    for k in range(1, 8):
        wp_copy(k).start()

    def w_place(yh_of):
        def place(pos, half):
            return w_ref.at[(pos * 2 + yh_of) * 2 + core, pl.ds(half * 48, 48), :]

        return place

    def l_place(yl_of):
        def place(pos, half):
            return l_ref.at[pos * 2 + yl_of, pl.ds(half * 96, 96), :]

        return place

    w_rings = [
        Ring(w_place(yh), x, x_up, x_down, send_sems, recv_sems, 0),
        Ring(w_place(1 - yh), x, x_up, x_down, send_sems, recv_sems, 6),
    ]
    l_rings = [
        Ring(l_place(yl), z, z_up, z_down, send_sems, recv_sems, 12),
        Ring(l_place(1 - yl), z, z_up, z_down, send_sems, recv_sems, 18),
    ]

    def w_own(half):
        return right_ref.at[pl.ds(half * 48, 48), :]

    def l_own(half):
        return left_ref.at[pl.ds(half * 96, 96), :]

    swaps = []

    def swap(src, dst, key, target):
        copy = remote(src, dst, send_sems.at[key], recv_sems.at[key], target)
        copy.start()
        swaps.append(copy)

    for half in range(2):
        w_rings[0].start(half, w_own)
        l_rings[0].start(half, l_own)
        swap(w_own(half), w_place(yh)(x, half), 24 + half, far)
        swap(l_own(half), l_place(yl)(z, half), 26 + half, near)

    def to_other(pos, yh_of, key):
        slot = w_ref.at[(pos * 2 + yh_of) * 2 + core]
        swap(slot, slot, key, other)

    def swapped(place, pos, half, key):
        ref = place(pos, half)
        remote(ref, ref, send_sems.at[key], recv_sems.at[key], other).wait_recv()

    own_w.wait()
    own_l.wait()
    put_l.start()
    put_w.start()
    swap(own_right, w_ref.at[r], 28, other)
    total_l = lp_ref[r]
    for k in range(1, 16):
        lp_copy(k).wait_recv()
    for k in range(1, 16):
        total_l = total_l + lp_in[lax.rem(r + 16 - k, 16)]
    total_w = wp_ref[c]
    for k in range(1, 8):
        wp_copy(k).wait_recv()
    for k in range(1, 8):
        total_w = total_w + wp_in[lax.rem(c + 8 - k, 8)]
    piece[pl.ds(0, 24), :] = total_l
    piece[pl.ds(24, 24), :] = total_w
    own_p = pltpu.make_async_copy(piece, p_ref.at[core, y, x, z], local_sems.at[2])
    own_p.start()

    pz = Ring(
        lambda pos, half: p_ref.at[core, y, x, pos, pl.ds(half * 24, 24), :],
        z, z_up, z_down, send_sems, recv_sems, 36,
    )
    px = Ring(
        lambda pos, half: p_ref.at[core, y, pos, pl.ds(half * 2, 2)],
        x, x_up, x_down, send_sems, recv_sems, 42,
    )
    py = Ring(
        lambda pos, half: p_ref.at[core, pos, pl.ds(half * 2, 2)],
        y, y_up, y_down, send_sems, recv_sems, 48,
    )
    for half in range(2):
        pz.start(half, lambda h: piece.at[pl.ds(h * 24, 24), :])
    pz.forward()
    own_p.wait()
    pz.finish_near()
    pz.finish_far()
    for half in range(2):
        px.start(half)
    px.forward()
    px.finish_near()
    px.finish_far()
    for half in range(2):
        py.start(half)

    w_rings[0].forward()
    l_rings[0].forward()
    for half in range(2):
        swapped(w_place(1 - yh), x, half, 24 + half)
        swapped(l_place(1 - yl), z, half, 26 + half)
    for half in range(2):
        w_rings[1].start(half)
        l_rings[1].start(half)
    py.forward()
    to_other(x, 1 - yh, 29)
    w_rings[0].finish_near()
    to_other(w_rings[0].pos(-1), yh, 30)
    to_other(w_rings[0].pos(1), yh, 31)
    py.finish_near()
    py.finish_far()
    swap(p_ref.at[core], p_ref.at[core], 54, other)
    w_rings[0].finish_far()
    to_other(w_rings[0].pos(2), yh, 32)
    w_rings[1].forward()
    l_rings[1].forward()
    w_rings[1].finish_near()
    to_other(w_rings[0].pos(-1), 1 - yh, 33)
    to_other(w_rings[0].pos(1), 1 - yh, 34)
    w_rings[1].finish_far()
    to_other(w_rings[0].pos(2), 1 - yh, 35)
    for ring in l_rings:
        ring.finish_near()
        ring.finish_far()

    def from_other(pos, yh_of, key):
        slot = w_ref.at[(pos * 2 + yh_of) * 2 + 1 - core]
        remote(slot, slot, send_sems.at[key], recv_sems.at[key], other).wait_recv()

    ring = w_rings[0]
    from_other(x, yh, 28)
    from_other(x, 1 - yh, 29)
    from_other(ring.pos(-1), yh, 30)
    from_other(ring.pos(1), yh, 31)
    from_other(ring.pos(2), yh, 32)
    from_other(ring.pos(-1), 1 - yh, 33)
    from_other(ring.pos(1), 1 - yh, 34)
    from_other(ring.pos(2), 1 - yh, 35)
    panels = p_ref.at[1 - core]
    remote(panels, panels, send_sems.at[54], recv_sems.at[54], other).wait_recv()

    put_l.wait()
    put_w.wait()
    for k in range(1, 16):
        lp_copy(k).wait_send()
    for k in range(1, 8):
        wp_copy(k).wait_send()
    for ring in w_rings + l_rings + [pz, px, py]:
        ring.drain()
    for copy in swaps:
        copy.wait_send()


def gather(left_t, right, lp, wp):
    any_spec = pl.BlockSpec(memory_space=pl.ANY)
    vmem_spec = pl.BlockSpec(memory_space=pltpu.VMEM)
    dma = pltpu.SemaphoreType.DMA
    return pl.pallas_call(
        gather_kernel,
        out_shape=(
            jax.ShapeDtypeStruct((8, 192, 1280), F32),
            jax.ShapeDtypeStruct((16, 96, 2560), F32),
            jax.ShapeDtypeStruct((2, 4, 4, 4, 48, 256), F32),
        ),
        in_specs=[any_spec, any_spec, vmem_spec, vmem_spec],
        out_specs=(any_spec, any_spec, any_spec),
        scratch_shapes=[
            pltpu.VMEM((16, 24, 256), F32),
            pltpu.VMEM((8, 24, 256), F32),
            pltpu.VMEM((48, 256), F32),
            dma((55,)),
            dma((55,)),
            dma((16,)),
            dma((16,)),
            dma((8,)),
            dma((8,)),
            dma((5,)),
            pltpu.VMEM((192, 1280), F32),
            pltpu.VMEM((96, 2560), F32),
        ],
        compiler_params=pltpu.CompilerParams(collective_id=0, has_side_effects=True),
        name="gather",
    )(left_t, right, lp, wp)


def split(a):
    hi = a.astype(BF)
    return hi, (a - hi.astype(F32)).astype(BF)

def dot3(a, b, dims=((1,), (0,))):
    def one(p, q):
        return lax.dot_general(p, q, (dims, ((), ())), preferred_element_type=F32)
    return one(a[0], b[0]) + one(a[0], b[1]) + one(a[1], b[0])

def product_kernel(where_ref, lt_ref, w_ref, lk_ref, e_ref, low_ref, screen_ref, o_ref, lh, ll):
    n = pl.program_id(0)
    @pl.when(n == 0)
    def _():
        e = split(e_ref[...])
        @pl.loop(0, 6)
        def _(k):
            at = pl.ds(pl.multiple_of(k * 256, 256), 256)
            lk = split(lk_ref[at, :])
            part = lt_ref[at, :].T - dot3(e, lk, ((1,), (1,)))
            hi, lo = split(part)
            lh[:, at] = hi
            ll[:, at] = lo
    w = split(w_ref[...])
    o_ref[...] = COUPLING * dot3((lh[...], ll[...]), w)
    row0 = where_ref[0] * 5
    block = where_ref[1] * 10 + n
    rel = block - row0
    @pl.when((rel >= 0) & (rel < 5))
    def _():
        at = pl.ds(pl.multiple_of(rel * PANEL, PANEL), PANEL)
        eye = (lax.broadcasted_iota(jnp.int32, (PANEL, PANEL), 0) == lax.broadcasted_iota(jnp.int32, (PANEL, PANEL), 1)).astype(F32)
        o_ref[at, :] += eye * screen_ref[rel]
    for s in range(2):
        @pl.when(block == where_ref[2 + s])
        def _():
            for m in range(5):
                hit = row0 + m == where_ref[2]
                if s == 1: hit = hit | (row0 + m == where_ref[3])
                @pl.when(jnp.logical_not(hit))
                def _():
                    at = pl.ds(m * PANEL, PANEL)
                    o_ref[at, :] = low_ref[at, s * PANEL:(s + 1) * PANEL]

def product(where, lt, w, lk, e, low, screen_rows):
    once = dict(pipeline_mode=pl.Buffered(1))
    return pl.pallas_call(product_kernel,
        out_shape=jax.ShapeDtypeStruct((1280, 2560), F32),
        grid_spec=pltpu.PrefetchScalarGridSpec(num_scalar_prefetch=1, grid=(10,),
            in_specs=[pl.BlockSpec((1536, 1280), lambda n, s: (0, 0), **once),
                      pl.BlockSpec((1536, 256), lambda n, s: (0, n)),
                      pl.BlockSpec((1536, 512), lambda n, s: (0, 0), **once),
                      pl.BlockSpec((1280, 512), lambda n, s: (0, 0), **once),
                      pl.BlockSpec((1280, 512), lambda n, s: (0, 0), **once),
                      pl.BlockSpec((5, 1, 256), lambda n, s: (0, 0, 0), **once)],
            out_specs=pl.BlockSpec((1280, 256), lambda n, s: (0, n)),
            scratch_shapes=[pltpu.VMEM((1280, 1536), BF), pltpu.VMEM((1280, 1536), BF)]),
        compiler_params=pltpu.CompilerParams(vmem_limit_bytes=56 << 20), name="product",
    )(where, lt, w, lk, e, low, screen_rows)


def dot(a, b, precision=lax.Precision.HIGH, dims=((1,), (0,))):
    return lax.dot_general(
        a, b, (dims, ((), ())), precision=precision, preferred_element_type=F32
    )


def newton_inverse(matrix_in):
    eye = jnp.eye(matrix_in.shape[0], dtype=F32)
    diagonal = jnp.sum(matrix_in * eye, axis=0)
    approx = eye / diagonal[None, :]
    for _ in range(NS_STEPS):
        product = dot(matrix_in, approx)
        approx = dot(approx, 2.0 * eye - product)
    return approx


def shards(left_pairs, right_pairs, pair_weight, screen, panel_index):
    left_t = left_pairs.T
    weighted = right_pairs * pair_weight[:, None]
    rows_here = left_pairs.shape[0]
    cols_here = weighted.shape[1]
    row_start = lax.axis_index("row") * rows_here
    col_start = lax.axis_index("col") * cols_here

    lp, wp = [], []
    for section in range(SECTIONS):
        anchor = panel_index[section] * PANEL
        at_row = anchor - row_start
        at_col = anchor - col_start
        here_row = (at_row >= 0) & (at_row < rows_here)
        here_col = (at_col >= 0) & (at_col < cols_here)
        part = lax.dynamic_slice_in_dim(left_t, jnp.clip(at_row, 0, rows_here - PANEL), PANEL, 1)
        lp.append(jnp.where(here_row, part, 0.0).reshape(8, 24, PANEL))
        part = lax.dynamic_slice_in_dim(weighted, jnp.clip(at_col, 0, cols_here - PANEL), PANEL, 1)
        wp.append(jnp.where(here_col, part, 0.0).reshape(4, 24, PANEL))
    lp = jnp.stack(lp, axis=1).reshape(16, 24, PANEL)
    wp = jnp.stack(wp, axis=1).reshape(8, 24, PANEL)

    l_all, w_all, panels = gather(left_t, weighted, lp, wp)
    lt = l_all.reshape(1536, rows_here)
    w = w_all.reshape(1536, cols_here)
    panels = panels.reshape(2, 2, 2, 4, 4, 2, 24, PANEL)
    lk_t = panels[:, :, :, :, :, 0].transpose(4, 2, 3, 1, 5, 0, 6).reshape(1536, 2 * PANEL)
    wk = panels[:, :, :, :, :, 1].transpose(3, 1, 0, 4, 5, 2, 6).reshape(1536, 2 * PANEL)

    glob_rows = row_start + jnp.arange(rows_here, dtype=jnp.int32)
    first, second = panel_index[0] * PANEL, panel_index[1] * PANEL

    def inside(positions, anchor):
        return (positions >= anchor) & (positions < anchor + PANEL)

    mask1 = jnp.logical_not(inside(glob_rows, first))
    mask2 = mask1 & jnp.logical_not(inside(glob_rows, second))
    eye = jnp.eye(PANEL, dtype=F32)
    screen1 = lax.dynamic_slice_in_dim(screen, first, PANEL, 0)
    screen2 = lax.dynamic_slice_in_dim(screen, second, PANEL, 0)

    x = COUPLING * dot(lk_t, wk, dims=((0,), (0,)))
    x11, x12 = x[:PANEL, :PANEL], x[:PANEL, PANEL:]
    x21, x22 = x[PANEL:, :PANEL], x[PANEL:, PANEL:]
    inv1 = newton_inverse(x11 + eye * screen1[None, :])
    b1 = dot(x21, inv1)
    inv2 = newton_inverse(x22 - dot(b1, x12) + eye * screen2[None, :])
    cols = COUPLING * dot(lt, wk, dims=((0,), (0,)))
    low1 = jnp.where(mask1[:, None], dot(cols[:, :PANEL], inv1), 0.0)
    low2 = jnp.where(mask2[:, None], dot(cols[:, PANEL:] - dot(low1, x12), inv2), 0.0)
    e = jnp.concatenate([low1 - dot(low2, b1), low2], axis=1)
    low = jnp.concatenate([low1, low2], axis=1)
    screen_rows = lax.dynamic_slice_in_dim(screen, row_start, rows_here, 0)
    where = jnp.stack(
        [lax.axis_index("row"), lax.axis_index("col"), panel_index[0], panel_index[1]]
    ).astype(jnp.int32)
    return product(where, lt, w, lk_t, e, low, screen_rows.reshape(5, 1, PANEL))


def solution(mesh):
    return jax.shard_map(
        shards,
        mesh=mesh,
        in_specs=(P("row", "col"), P("row", "col"), P("row"), P(), P()),
        out_specs=P("row", "col"),
        check_vma=False,
    )
```

```python
import jax
import jax.numpy as jnp
from jax import lax
from jax.experimental import pallas as pl
from jax.experimental.pallas import tpu as pltpu
from jax.sharding import PartitionSpec as P

PANEL = 256
SECTIONS = 2
NS_STEPS = 3

COUPLING = 0.08

SCHEDULE = (
    "p", "wy", "ly", "w0", "l0", "p", "p", "p", "wy", "ly",
    "w0", "l0", "p", "w0", "l0", "w1", "l1", "p", "w1", "l1",
    "p", "p", "p", "w0", "p", "w0", "w1", "l1", "p", "t",
    "chain", "w1", "w1", "t", "chain",
)

MESH = pl.DeviceIdType.MESH
F32 = jnp.float32
BF = jnp.bfloat16


def remote(src, dst, send_sem, recv_sem, target):
    return pltpu.make_async_remote_copy(
        src_ref=src,
        dst_ref=dst,
        send_sem=send_sem,
        recv_sem=recv_sem,
        device_id=target,
        device_id_type=MESH,
    )


class Ring:
    def __init__(self, ref, me, ahead, behind, send_sems, recv_sems, base):
        self.ref, self.me = ref, me
        self.ahead, self.behind = ahead, behind
        self.send_sems, self.recv_sems, self.base = send_sems, recv_sems, base
        self.sent = []

    def pos(self, step):
        return lax.rem(self.me + 4 + step, 4)

    def send(self, src, pos, half, key, target):
        copy = remote(
            src,
            self.ref(pos, half),
            self.send_sems.at[self.base + key],
            self.recv_sems.at[self.base + key],
            target,
        )
        copy.start()
        self.sent.append(copy)

    def arrived(self, pos, half, key):
        ref = self.ref(pos, half)
        remote(
            ref,
            ref,
            self.send_sems.at[self.base + key],
            self.recv_sems.at[self.base + key],
            self.ahead,
        ).wait_recv()

    def start(self, half_at, source=None):
        source = source or (lambda half: self.ref(self.me, half))
        first, second = (0, 1) if half_at == 0 else (1, 0)
        self.send(source(first), self.me, first, first, self.ahead)
        self.send(source(second), self.me, second, 2 + second, self.behind)

    def forward(self):
        self.arrived(self.pos(-1), 0, 0)
        self.send(self.ref(self.pos(-1), 0), self.pos(-1), 0, 4, self.ahead)
        self.arrived(self.pos(1), 1, 3)
        self.send(self.ref(self.pos(1), 1), self.pos(1), 1, 5, self.behind)

    def finish_near(self):
        self.arrived(self.pos(-1), 1, 1)
        self.arrived(self.pos(1), 0, 2)

    def finish_far(self):
        self.arrived(self.pos(2), 0, 4)
        self.arrived(self.pos(2), 1, 5)

    def drain(self):
        for copy in self.sent:
            copy.wait_send()


def split(a):
    hi = a.astype(BF)
    return hi, (a - hi.astype(F32)).astype(BF)


def dot3(a, b, dims=((1,), (0,))):
    def one(p, q):
        return lax.dot_general(p, q, (dims, ((), ())), preferred_element_type=F32)

    return one(a[0], b[0]) + one(a[0], b[1]) + one(a[1], b[0])


def unit():
    rows = lax.broadcasted_iota(jnp.int32, (PANEL, PANEL), 0)
    cols = lax.broadcasted_iota(jnp.int32, (PANEL, PANEL), 1)
    return (rows == cols).astype(F32)


def newton_inverse(matrix_in):
    eye = unit()
    approx = eye / jnp.sum(matrix_in * eye, axis=0, keepdims=True)
    whole = split(matrix_in)
    for _ in range(NS_STEPS):
        now = split(approx)
        product = dot3(whole, now)
        approx = dot3(now, split(2.0 * eye - product))
    return approx


def gather_kernel(
    left_ref,
    right_ref,
    index_ref,
    screen_ref,
    w_ref,
    high_ref,
    low_ref,
    lower_ref,
    lt,
    p_ref,
    lkt,
    wk,
    lh,
    ll,
    cc,
    lower,
    eh,
    el,
    mids,
    lp_ref,
    wp_ref,
    lp_in,
    wp_in,
    piece,
    own_left,
    own_right,
    send_sems,
    recv_sems,
    lps_sems,
    lpr_sems,
    wps_sems,
    wpr_sems,
    local_sems,
    left_sems,
):
    r = lax.axis_index("row")
    c = lax.axis_index("col")
    core = lax.rem(r, 2)
    yh = lax.rem(r // 2, 2)
    x = r // 4
    yl = lax.rem(c, 2)
    z = c // 2
    y = yh * 2 + yl

    def at(x=x, y=y, z=z, core=core):
        return {"row": (x * 2 + y // 2) * 2 + core, "col": z * 2 + lax.rem(y, 2)}

    x_up, x_down = at(x=lax.rem(x + 1, 4)), at(x=lax.rem(x + 3, 4))
    z_up, z_down = at(z=lax.rem(z + 1, 4)), at(z=lax.rem(z + 3, 4))
    far = at(y=lax.rem(y + 2, 4))
    near = at(y=yh * 2 + 1 - yl)
    other = at(core=1 - core)

    def l_slot(slot, half):
        return lt.at[pl.ds(pl.multiple_of(slot * 192 + half * 96, 96), 96), :]

    own_l = pltpu.make_async_copy(left_ref, own_left, local_sems.at[0])
    own_w = pltpu.make_async_copy(right_ref, own_right, local_sems.at[1])
    own_l.start()
    own_w.start()
    put_w = pltpu.make_async_copy(own_right, w_ref.at[r], local_sems.at[3])
    put_l = pltpu.make_async_copy(
        own_left, lt.at[pl.ds(pl.multiple_of(c * 192, 192), 192), :], local_sems.at[5]
    )

    barrier = pltpu.get_barrier_semaphore()

    def greet_row(k, carry):
        pl.semaphore_signal(
            barrier, 1, device_id={"row": lax.rem(r + k, 16), "col": c}, device_id_type=MESH
        )
        return carry

    def greet_col(k, carry):
        pl.semaphore_signal(
            barrier, 1, device_id={"row": r, "col": lax.rem(c + k, 8)}, device_id_type=MESH
        )
        return carry

    lax.fori_loop(1, 16, greet_row, 0)
    lax.fori_loop(1, 8, greet_col, 0)
    across = at(y=lax.rem(y + 3 + 2 * yl, 4))
    pl.semaphore_signal(barrier, 1, device_id=across, device_id_type=MESH)

    def hit(s, block):
        return jnp.where(index_ref[s : s + 1, :] == block, 1.0, 0.0)

    own_l.wait()
    own_w.wait()
    put_l.start()
    put_w.start()
    for s in range(SECTIONS):
        part = jnp.zeros((192, PANEL), F32)
        for b in range(5):
            part = part + own_left[:, b * PANEL : (b + 1) * PANEL] * hit(s, r * 5 + b)
        for g in range(8):
            lp_ref[g * 2 + s] = part[g * 24 : g * 24 + 24]
        part = jnp.zeros((96, PANEL), F32)
        for b in range(10):
            part = part + own_right[:, b * PANEL : (b + 1) * PANEL] * hit(s, c * 10 + b)
        for g in range(4):
            wp_ref[g * 2 + s] = part[g * 24 : g * 24 + 24]
    pl.semaphore_wait(barrier, 23)

    def lp_copy(k):
        to = lax.rem(r + k, 16)
        return remote(
            lp_ref.at[to], lp_in.at[r], lps_sems.at[k], lpr_sems.at[k], {"row": to, "col": c}
        )

    def wp_copy(k):
        to = lax.rem(c + k, 8)
        return remote(
            wp_ref.at[to], wp_in.at[c], wps_sems.at[k], wpr_sems.at[k], {"row": r, "col": to}
        )

    def w_place(yh_of):
        return lambda pos, half: w_ref.at[(pos * 2 + yh_of) * 2 + core, pl.ds(half * 48, 48), :]

    def l_place(yl_of):
        return lambda pos, half: l_slot(pos * 2 + yl_of, half)

    w_rings = [
        Ring(w_place(yh), x, x_up, x_down, send_sems, recv_sems, 0),
        Ring(w_place(1 - yh), x, x_up, x_down, send_sems, recv_sems, 6),
    ]
    l_rings = [
        Ring(l_place(yl), z, z_up, z_down, send_sems, recv_sems, 12),
        Ring(l_place(1 - yl), z, z_up, z_down, send_sems, recv_sems, 18),
    ]
    pz = Ring(
        lambda pos, half: p_ref.at[core, y, x, pos, pl.ds(half * 24, 24), :],
        z, z_up, z_down, send_sems, recv_sems, 36,
    )
    px = Ring(
        lambda pos, half: p_ref.at[core, y, pos, pl.ds(half * 2, 2)],
        x, x_up, x_down, send_sems, recv_sems, 42,
    )
    spots = [x, px.pos(-1), px.pos(1), px.pos(2)]

    def w_own(half):
        return right_ref.at[pl.ds(half * 48, 48), :]

    def l_own(half):
        return left_ref.at[pl.ds(half * 96, 96), :]

    swaps = []

    def swap(src, dst, key, target):
        copy = remote(src, dst, send_sems.at[key], recv_sems.at[key], target)
        copy.start()
        swaps.append(copy)

    def to_other(pos, yh_of, key):
        slot = w_ref.at[(pos * 2 + yh_of) * 2 + core]
        swap(slot, slot, key, other)

    def arrived(ref, key):
        remote(ref, ref, send_sems.at[key], recv_sems.at[key], other).wait_recv()

    def from_other(pos, yh_of, key):
        arrived(w_ref.at[(pos * 2 + yh_of) * 2 + 1 - core], key)

    def flow_w0():
        ring = w_rings[0]
        ring.start(0, w_own)
        yield
        ring.start(1, w_own)
        yield
        swap(own_right, w_ref.at[r], 28, other)
        ring.forward()
        yield
        ring.finish_near()
        to_other(ring.pos(-1), yh, 30)
        to_other(ring.pos(1), yh, 31)
        yield
        ring.finish_far()
        to_other(ring.pos(2), yh, 32)
        yield

    def flow_wy():
        for half in range(2):
            swap(w_own(half), w_place(yh)(x, half), 24 + half, far)
            yield

    def follow(ring, place, me, key):
        for half in range(2):
            ref = place(me, half)
            arrived(ref, key + half)
            ring.send(ref, me, half, half, ring.ahead)
            ring.send(ref, me, half, 2 + half, ring.behind)
            yield

    def flow_w1():
        ring = w_rings[1]
        yield from follow(ring, w_place(1 - yh), x, 24)
        to_other(x, 1 - yh, 29)
        ring.forward()
        yield
        ring.finish_near()
        to_other(ring.pos(-1), 1 - yh, 33)
        to_other(ring.pos(1), 1 - yh, 34)
        yield
        ring.finish_far()
        to_other(ring.pos(2), 1 - yh, 35)
        yield

    def flow_l0():
        ring = l_rings[0]
        ring.start(0, l_own)
        yield
        ring.start(1, l_own)
        yield
        ring.forward()
        yield

    def flow_ly():
        for half in range(2):
            swap(l_own(half), l_place(yl)(z, half), 26 + half, near)
            yield

    def flow_l1():
        ring = l_rings[1]
        yield from follow(ring, l_place(1 - yl), z, 26)
        ring.forward()
        yield

    def turn(pos):
        at_k = pl.ds(pl.multiple_of(pos * 384, 384), 384)

        @pl.loop(0, 5)
        def _(m):
            at_m = pl.ds(pl.multiple_of(m * PANEL, PANEL), PANEL)
            hi, lo = split(lt[at_k, at_m].T)
            lh[at_m, at_k] = hi
            ll[at_m, at_k] = lo

    def flow_t():
        put_l.wait()
        for ring in l_rings:
            ring.finish_near()
        for step in (0, -1, 1):
            turn(l_rings[0].pos(step))
        yield
        for ring in l_rings:
            ring.finish_far()
        turn(l_rings[0].pos(2))
        yield

    def flow_p():
        for k in range(1, 16):
            lp_copy(k).start()
        for k in range(1, 8):
            wp_copy(k).start()
        yield
        total_l = lp_ref[r]
        for k in range(1, 16):
            lp_copy(k).wait_recv()
        for k in range(1, 16):
            total_l = total_l + lp_in[lax.rem(r + 16 - k, 16)]
        total_w = wp_ref[c]
        for k in range(1, 8):
            wp_copy(k).wait_recv()
        for k in range(1, 8):
            total_w = total_w + wp_in[lax.rem(c + 8 - k, 8)]
        piece[pl.ds(0, 24), :] = total_l
        piece[pl.ds(24, 24), :] = total_w
        own_p = pltpu.make_async_copy(piece, p_ref.at[core, y, x, z], local_sems.at[2])
        own_p.start()
        for half in range(2):
            pz.start(half, lambda h: piece.at[pl.ds(h * 24, 24), :])
        yield
        pz.forward()
        yield
        def slot(y_of, i):
            return p_ref.at[core, y_of, spots[i]]

        def go(i):
            swap(slot(y, i), slot(y, i), 55 + 3 * i, near)
            swap(slot(y, i), slot(y, i), 56 + 3 * i, across)

        def onward(i):
            ref = slot(yh * 2 + 1 - yl, i)
            arrived(ref, 55 + 3 * i)
            swap(ref, ref, 57 + 3 * i, across)

        def share(i):
            arrived(slot(lax.rem(y + 3 + 2 * yl, 4), i), 56 + 3 * i)
            arrived(slot(lax.rem(y + 2, 4), i), 57 + 3 * i)
            whole = p_ref.at[core, pl.ds(0, 4), spots[i]]
            swap(whole, whole, 67 + i, other)

        own_p.wait()
        pz.finish_near()
        pz.finish_far()
        for half in range(2):
            px.start(half)
        go(0)
        yield
        px.forward()
        yield
        px.finish_near()
        go(1)
        go(2)
        onward(0)
        yield
        px.finish_far()
        go(3)
        onward(1)
        onward(2)
        yield
        share(0)
        onward(3)
        yield
        share(1)
        share(2)
        yield
        share(3)
        yield
        for i in range(4):
            arrived(p_ref.at[1 - core, pl.ds(0, 4), spots[i]], 67 + i)
        place_panels()
        yield

    def place_panels():
        @pl.loop(0, 32)
        def _(i):
            x_of, yh_of, z_of = i // 8, lax.rem(i // 4, 2), lax.rem(i, 4)
            for core_of in range(2):
                for yl_of in range(2):
                    block = p_ref[core_of, yh_of * 2 + yl_of, x_of, z_of]
                    at_l = pl.multiple_of((z_of * 2 + yl_of) * 192 + (x_of * 2 + yh_of) * 24, 24)
                    at_w = pl.multiple_of(
                        ((x_of * 2 + yh_of) * 2 + core_of) * 96 + z_of * 24, 24
                    )
                    lkt[pl.ds(at_l, 24), pl.ds(core_of * PANEL, PANEL)] = block[:24]
                    wk[pl.ds(at_w, 24), pl.ds(yl_of * PANEL, PANEL)] = block[24:]

    first, second = pl.ds(0, PANEL), pl.ds(PANEL, PANEL)

    def flow_chain():
        mids[...] = jnp.zeros_like(mids)

        @pl.loop(0, 6)
        def _(k):
            at_k = pl.ds(pl.multiple_of(k * PANEL, PANEL), PANEL)
            mids[...] += COUPLING * dot3(split(lkt[at_k, :].T), split(wk[at_k, :]))

        def screened(block, s):
            places = lax.broadcasted_iota(jnp.int32, (80, PANEL), 0)
            chosen = jnp.where(places == index_ref[s : s + 1, :], screen_ref[...], 0.0)
            return block + unit() * jnp.sum(chosen, axis=0, keepdims=True)

        inv1 = split(newton_inverse(screened(mids[first, first], 0)))
        x12 = split(mids[first, second])
        b1 = split(dot3(split(mids[second, first]), inv1))
        inv2 = split(newton_inverse(screened(mids[second, second] - dot3(b1, x12), 1)))
        yield
        for half in (first, second):
            cc[:, half] = COUPLING * dot3((lh[...], ll[...]), split(wk[:, half]))

        @pl.loop(0, 5)
        def _(m):
            at_m = pl.ds(pl.multiple_of(m * PANEL, PANEL), PANEL)
            mask1 = 1.0 - hit(0, r * 5 + m)
            mask2 = mask1 * (1.0 - hit(1, r * 5 + m))
            low1 = dot3(split(cc[at_m, first]), inv1) * mask1
            low2 = cc[at_m, second] - dot3(split(low1), x12)
            low2 = dot3(split(low2), inv2) * mask2
            lower[at_m, first] = low1
            lower[at_m, second] = low2
            pair = split(low2)
            eh[at_m, second], el[at_m, second] = pair
            eh[at_m, first], el[at_m, first] = split(low1 - dot3(pair, b1))

        put_lower.start()

        @pl.loop(0, 6)
        def _(k):
            at_k = pl.ds(pl.multiple_of(k * PANEL, PANEL), PANEL)
            panel = split(lkt[at_k, :])
            now = lh[:, at_k].astype(F32) + ll[:, at_k].astype(F32)
            now = now - dot3((eh[...], el[...]), panel, ((1,), (1,)))
            lh[:, at_k], ll[:, at_k] = split(now)
            for put in put_left(k):
                put.start()

        yield

    def put_left(k):
        at_k = pl.ds(pl.multiple_of(k * PANEL, PANEL), PANEL)
        return (
            pltpu.make_async_copy(lh.at[:, at_k], high_ref.at[:, at_k], left_sems.at[0, k]),
            pltpu.make_async_copy(ll.at[:, at_k], low_ref.at[:, at_k], left_sems.at[1, k]),
        )

    put_lower = pltpu.make_async_copy(lower, lower_ref, local_sems.at[4])

    makers = {
        "w0": flow_w0, "wy": flow_wy, "w1": flow_w1, "l0": flow_l0, "ly": flow_ly,
        "l1": flow_l1, "p": flow_p, "t": flow_t, "chain": flow_chain,
    }
    flows = {}
    for name in SCHEDULE:
        if name not in flows:
            flows[name] = makers[name]()
        next(flows[name])
    for flow in flows.values():
        for _ in flow:
            pass

    ring = w_rings[0]
    from_other(x, yh, 28)
    from_other(x, 1 - yh, 29)
    from_other(ring.pos(-1), yh, 30)
    from_other(ring.pos(1), yh, 31)
    from_other(ring.pos(2), yh, 32)
    from_other(ring.pos(-1), 1 - yh, 33)
    from_other(ring.pos(1), 1 - yh, 34)
    from_other(ring.pos(2), 1 - yh, 35)
    put_w.wait()
    put_lower.wait()
    for k in range(6):
        for put in put_left(k):
            put.wait()
    for k in range(1, 16):
        lp_copy(k).wait_send()
    for k in range(1, 8):
        wp_copy(k).wait_send()
    for ring in w_rings + l_rings + [pz, px]:
        ring.drain()
    for copy in swaps:
        copy.wait_send()


def gather(left_t, right, index, screen):
    any_spec = pl.BlockSpec(memory_space=pl.ANY)
    vmem_spec = pl.BlockSpec(memory_space=pltpu.VMEM)
    dma = pltpu.SemaphoreType.DMA
    return pl.pallas_call(
        gather_kernel,
        out_shape=(
            jax.ShapeDtypeStruct((16, 96, 2560), F32),
            jax.ShapeDtypeStruct((1280, 1536), BF),
            jax.ShapeDtypeStruct((1280, 1536), BF),
            jax.ShapeDtypeStruct((1280, 512), F32),
        ),
        in_specs=[any_spec, any_spec, vmem_spec, vmem_spec],
        out_specs=(any_spec, any_spec, any_spec, any_spec),
        scratch_shapes=[
            pltpu.VMEM((1536, 1280), F32),
            pltpu.VMEM((2, 4, 4, 4, 48, PANEL), F32),
            pltpu.VMEM((1536, 512), F32),
            pltpu.VMEM((1536, 512), F32),
            pltpu.VMEM((1280, 1536), BF),
            pltpu.VMEM((1280, 1536), BF),
            pltpu.VMEM((1280, 512), F32),
            pltpu.VMEM((1280, 512), F32),
            pltpu.VMEM((1280, 512), BF),
            pltpu.VMEM((1280, 512), BF),
            pltpu.VMEM((512, 512), F32),
            pltpu.VMEM((16, 24, PANEL), F32),
            pltpu.VMEM((8, 24, PANEL), F32),
            pltpu.VMEM((16, 24, PANEL), F32),
            pltpu.VMEM((8, 24, PANEL), F32),
            pltpu.VMEM((48, PANEL), F32),
            pltpu.VMEM((192, 1280), F32),
            pltpu.VMEM((96, 2560), F32),
            dma((71,)),
            dma((71,)),
            dma((16,)),
            dma((16,)),
            dma((8,)),
            dma((8,)),
            dma((6,)),
            dma((2, 6)),
        ],
        compiler_params=pltpu.CompilerParams(
            collective_id=0, has_side_effects=True, vmem_limit_bytes=58 << 20
        ),
        name="exchange",
    )(left_t, right, index, screen)


def product_kernel(index_ref, lh_ref, ll_ref, w_ref, lower_ref, screen_ref, o_ref):
    n = pl.program_id(0)
    w = split(w_ref[...])
    o_ref[...] = COUPLING * dot3((lh_ref[...], ll_ref[...]), w)
    row0 = lax.axis_index("row") * 5
    block = lax.axis_index("col") * 10 + n
    rel = block - row0

    @pl.when((rel >= 0) & (rel < 5))
    def _():
        at = pl.ds(pl.multiple_of(rel * PANEL, PANEL), PANEL)
        o_ref[at, :] += unit() * screen_ref[pl.ds(block, 1), :]

    for s in range(2):

        @pl.when(block == index_ref[s])
        def _():
            for m in range(5):
                hit = row0 + m == index_ref[0]
                if s == 1:
                    hit = hit | (row0 + m == index_ref[1])

                @pl.when(jnp.logical_not(hit))
                def _():
                    at = pl.ds(m * PANEL, PANEL)
                    o_ref[at, :] = lower_ref[at, s * PANEL : (s + 1) * PANEL]


def product(index, lh, ll, w, lower, screen):
    once = dict(pipeline_mode=pl.Buffered(1))
    return pl.pallas_call(
        product_kernel,
        out_shape=jax.ShapeDtypeStruct((1280, 2560), F32),
        grid_spec=pltpu.PrefetchScalarGridSpec(
            num_scalar_prefetch=1,
            grid=(10,),
            in_specs=[
                pl.BlockSpec((1280, 1536), lambda n, s: (0, 0), **once),
                pl.BlockSpec((1280, 1536), lambda n, s: (0, 0), **once),
                pl.BlockSpec((1536, PANEL), lambda n, s: (0, n)),
                pl.BlockSpec((1280, 512), lambda n, s: (0, 0), **once),
                pl.BlockSpec((80, PANEL), lambda n, s: (0, 0), **once),
            ],
            out_specs=pl.BlockSpec((1280, PANEL), lambda n, s: (0, n)),
        ),
        compiler_params=pltpu.CompilerParams(vmem_limit_bytes=56 << 20),
        name="product",
    )(index, lh, ll, w, lower, screen)


def shards(left_pairs, right_pairs, pair_weight, screen, panel_index):
    weighted = right_pairs * pair_weight[:, None]
    screen = screen.reshape(80, PANEL)
    index = jnp.broadcast_to(panel_index[:, None], (SECTIONS, PANEL))
    w_all, lh, ll, lower = gather(left_pairs.T, weighted, index, screen)
    return product(panel_index, lh, ll, w_all.reshape(1536, 2560), lower, screen)


def solution(mesh):
    return jax.shard_map(
        shards,
        mesh=mesh,
        in_specs=(P("row", "col"), P("row", "col"), P("row"), P(), P()),
        out_specs=P("row", "col"),
        check_vma=False,
    )
```

```python
import jax
import jax.numpy as jnp
from jax import lax
from jax.experimental import pallas as pl
from jax.experimental.pallas import tpu as pltpu
from jax.sharding import PartitionSpec as P

PANEL = 256
SECTIONS = 2
NS_STEPS = 3

COUPLING = 0.08

SCHEDULE = (
    "p", "wy", "ly", "w0", "l0", "p", "p", "p", "wy", "ly",
    "w0", "l0", "p", "w0", "l0", "w1", "l1", "p", "w1", "l1",
    "p", "p", "p", "w0", "p", "w0", "w1", "l1", "p", "t",
    "c", "c", "p", "c", "p", "chain", "w1", "w1", "t", "c",
    "chain",
)

MESH = pl.DeviceIdType.MESH
F32 = jnp.float32
BF = jnp.bfloat16


def remote(src, dst, send_sem, recv_sem, target):
    return pltpu.make_async_remote_copy(
        src_ref=src,
        dst_ref=dst,
        send_sem=send_sem,
        recv_sem=recv_sem,
        device_id=target,
        device_id_type=MESH,
    )


class Ring:
    def __init__(self, ref, me, ahead, behind, send_sems, recv_sems, base):
        self.ref, self.me = ref, me
        self.ahead, self.behind = ahead, behind
        self.send_sems, self.recv_sems, self.base = send_sems, recv_sems, base
        self.sent = []

    def pos(self, step):
        return lax.rem(self.me + 4 + step, 4)

    def send(self, src, pos, half, key, target):
        copy = remote(
            src,
            self.ref(pos, half),
            self.send_sems.at[self.base + key],
            self.recv_sems.at[self.base + key],
            target,
        )
        copy.start()
        self.sent.append(copy)

    def arrived(self, pos, half, key):
        ref = self.ref(pos, half)
        remote(
            ref,
            ref,
            self.send_sems.at[self.base + key],
            self.recv_sems.at[self.base + key],
            self.ahead,
        ).wait_recv()

    def start(self, half_at, source=None):
        source = source or (lambda half: self.ref(self.me, half))
        first, second = (0, 1) if half_at == 0 else (1, 0)
        self.send(source(first), self.me, first, first, self.ahead)
        self.send(source(second), self.me, second, 2 + second, self.behind)

    def forward(self):
        self.arrived(self.pos(-1), 0, 0)
        self.send(self.ref(self.pos(-1), 0), self.pos(-1), 0, 4, self.ahead)
        self.arrived(self.pos(1), 1, 3)
        self.send(self.ref(self.pos(1), 1), self.pos(1), 1, 5, self.behind)

    def finish_near(self):
        self.arrived(self.pos(-1), 1, 1)
        self.arrived(self.pos(1), 0, 2)

    def finish_far(self):
        self.arrived(self.pos(2), 0, 4)
        self.arrived(self.pos(2), 1, 5)

    def drain(self):
        for copy in self.sent:
            copy.wait_send()


def split(a):
    hi = a.astype(BF)
    return hi, (a - hi.astype(F32)).astype(BF)


def dot3(a, b, dims=((1,), (0,))):
    def one(p, q):
        return lax.dot_general(p, q, (dims, ((), ())), preferred_element_type=F32)

    return one(a[0], b[0]) + one(a[0], b[1]) + one(a[1], b[0])


def unit():
    rows = lax.broadcasted_iota(jnp.int32, (PANEL, PANEL), 0)
    cols = lax.broadcasted_iota(jnp.int32, (PANEL, PANEL), 1)
    return (rows == cols).astype(F32)


def newton_inverse(matrix_in):
    eye = unit()
    approx = eye / jnp.sum(matrix_in * eye, axis=0, keepdims=True)
    whole = split(matrix_in)
    for _ in range(NS_STEPS):
        now = split(approx)
        product = dot3(whole, now)
        approx = dot3(now, split(2.0 * eye - product))
    return approx


def gather_kernel(
    left_ref,
    right_ref,
    index_ref,
    screen_ref,
    w_ref,
    high_ref,
    low_ref,
    lower_ref,
    lt,
    p_ref,
    lkt,
    wk,
    lh,
    ll,
    cc,
    lower,
    eh,
    el,
    mids,
    lp_ref,
    wp_ref,
    lp_in,
    wp_in,
    piece,
    own_left,
    own_right,
    send_sems,
    recv_sems,
    lps_sems,
    lpr_sems,
    wps_sems,
    wpr_sems,
    local_sems,
    left_sems,
):
    r = lax.axis_index("row")
    c = lax.axis_index("col")
    core = lax.rem(r, 2)
    yh = lax.rem(r // 2, 2)
    x = r // 4
    yl = lax.rem(c, 2)
    z = c // 2
    y = yh * 2 + yl

    def at(x=x, y=y, z=z, core=core):
        return {"row": (x * 2 + y // 2) * 2 + core, "col": z * 2 + lax.rem(y, 2)}

    x_up, x_down = at(x=lax.rem(x + 1, 4)), at(x=lax.rem(x + 3, 4))
    z_up, z_down = at(z=lax.rem(z + 1, 4)), at(z=lax.rem(z + 3, 4))
    far = at(y=lax.rem(y + 2, 4))
    near = at(y=yh * 2 + 1 - yl)
    other = at(core=1 - core)

    def l_slot(slot, half):
        return lt.at[pl.ds(pl.multiple_of(slot * 192 + half * 96, 96), 96), :]

    own_l = pltpu.make_async_copy(left_ref, own_left, local_sems.at[0])
    own_w = pltpu.make_async_copy(right_ref, own_right, local_sems.at[1])
    own_l.start()
    own_w.start()
    put_w = pltpu.make_async_copy(own_right, w_ref.at[r], local_sems.at[3])
    put_l = pltpu.make_async_copy(
        own_left, lt.at[pl.ds(pl.multiple_of(c * 192, 192), 192), :], local_sems.at[5]
    )

    barrier = pltpu.get_barrier_semaphore()

    def greet_row(k, carry):
        pl.semaphore_signal(
            barrier, 1, device_id={"row": lax.rem(r + k, 16), "col": c}, device_id_type=MESH
        )
        return carry

    def greet_col(k, carry):
        pl.semaphore_signal(
            barrier, 1, device_id={"row": r, "col": lax.rem(c + k, 8)}, device_id_type=MESH
        )
        return carry

    lax.fori_loop(1, 16, greet_row, 0)
    lax.fori_loop(1, 8, greet_col, 0)
    across = at(y=lax.rem(y + 3 + 2 * yl, 4))
    pl.semaphore_signal(barrier, 1, device_id=across, device_id_type=MESH)

    def hit(s, block):
        return jnp.where(index_ref[s : s + 1, :] == block, 1.0, 0.0)

    own_l.wait()
    own_w.wait()
    put_l.start()
    put_w.start()
    for s in range(SECTIONS):
        part = jnp.zeros((192, PANEL), F32)
        for b in range(5):
            part = part + own_left[:, b * PANEL : (b + 1) * PANEL] * hit(s, r * 5 + b)
        for g in range(8):
            lp_ref[g * 2 + s] = part[g * 24 : g * 24 + 24]
        part = jnp.zeros((96, PANEL), F32)
        for b in range(10):
            part = part + own_right[:, b * PANEL : (b + 1) * PANEL] * hit(s, c * 10 + b)
        for g in range(4):
            wp_ref[g * 2 + s] = part[g * 24 : g * 24 + 24]
    pl.semaphore_wait(barrier, 23)

    def lp_copy(k):
        to = lax.rem(r + k, 16)
        return remote(
            lp_ref.at[to], lp_in.at[r], lps_sems.at[k], lpr_sems.at[k], {"row": to, "col": c}
        )

    def wp_copy(k):
        to = lax.rem(c + k, 8)
        return remote(
            wp_ref.at[to], wp_in.at[c], wps_sems.at[k], wpr_sems.at[k], {"row": r, "col": to}
        )

    def w_place(yh_of):
        return lambda pos, half: w_ref.at[(pos * 2 + yh_of) * 2 + core, pl.ds(half * 48, 48), :]

    def l_place(yl_of):
        return lambda pos, half: l_slot(pos * 2 + yl_of, half)

    w_rings = [
        Ring(w_place(yh), x, x_up, x_down, send_sems, recv_sems, 0),
        Ring(w_place(1 - yh), x, x_up, x_down, send_sems, recv_sems, 6),
    ]
    l_rings = [
        Ring(l_place(yl), z, z_up, z_down, send_sems, recv_sems, 12),
        Ring(l_place(1 - yl), z, z_up, z_down, send_sems, recv_sems, 18),
    ]
    pz = Ring(
        lambda pos, half: p_ref.at[core, y, x, pos, pl.ds(half * 24, 24), :],
        z, z_up, z_down, send_sems, recv_sems, 36,
    )
    px = Ring(
        lambda pos, half: p_ref.at[core, y, pos, pl.ds(half * 2, 2)],
        x, x_up, x_down, send_sems, recv_sems, 42,
    )
    spots = [x, px.pos(-1), px.pos(1), px.pos(2)]

    def w_own(half):
        return right_ref.at[pl.ds(half * 48, 48), :]

    def l_own(half):
        return left_ref.at[pl.ds(half * 96, 96), :]

    swaps = []

    def swap(src, dst, key, target):
        copy = remote(src, dst, send_sems.at[key], recv_sems.at[key], target)
        copy.start()
        swaps.append(copy)

    def to_other(pos, yh_of, key):
        slot = w_ref.at[(pos * 2 + yh_of) * 2 + core]
        swap(slot, slot, key, other)

    def arrived(ref, key):
        remote(ref, ref, send_sems.at[key], recv_sems.at[key], other).wait_recv()

    def from_other(pos, yh_of, key):
        arrived(w_ref.at[(pos * 2 + yh_of) * 2 + 1 - core], key)

    def flow_w0():
        ring = w_rings[0]
        ring.start(0, w_own)
        yield
        ring.start(1, w_own)
        yield
        swap(own_right, w_ref.at[r], 28, other)
        ring.forward()
        yield
        ring.finish_near()
        to_other(ring.pos(-1), yh, 30)
        to_other(ring.pos(1), yh, 31)
        yield
        ring.finish_far()
        to_other(ring.pos(2), yh, 32)
        yield

    def flow_wy():
        for half in range(2):
            swap(w_own(half), w_place(yh)(x, half), 24 + half, far)
            yield

    def follow(ring, place, me, key):
        for half in range(2):
            ref = place(me, half)
            arrived(ref, key + half)
            ring.send(ref, me, half, half, ring.ahead)
            ring.send(ref, me, half, 2 + half, ring.behind)
            yield

    def flow_w1():
        ring = w_rings[1]
        yield from follow(ring, w_place(1 - yh), x, 24)
        to_other(x, 1 - yh, 29)
        ring.forward()
        yield
        ring.finish_near()
        to_other(ring.pos(-1), 1 - yh, 33)
        to_other(ring.pos(1), 1 - yh, 34)
        yield
        ring.finish_far()
        to_other(ring.pos(2), 1 - yh, 35)
        yield

    def flow_l0():
        ring = l_rings[0]
        ring.start(0, l_own)
        yield
        ring.start(1, l_own)
        yield
        ring.forward()
        yield

    def flow_ly():
        for half in range(2):
            swap(l_own(half), l_place(yl)(z, half), 26 + half, near)
            yield

    def flow_l1():
        ring = l_rings[1]
        yield from follow(ring, l_place(1 - yl), z, 26)
        ring.forward()
        yield

    def turn(pos):
        at_k = pl.ds(pl.multiple_of(pos * 384, 384), 384)

        @pl.loop(0, 5)
        def _(m):
            at_m = pl.ds(pl.multiple_of(m * PANEL, PANEL), PANEL)
            hi, lo = split(lt[at_k, at_m].T)
            lh[at_m, at_k] = hi
            ll[at_m, at_k] = lo

    def flow_t():
        put_l.wait()
        for ring in l_rings:
            ring.finish_near()
        for step in (0, -1, 1):
            turn(l_rings[0].pos(step))
        yield
        for ring in l_rings:
            ring.finish_far()
        turn(l_rings[0].pos(2))
        yield

    def flow_p():
        for k in range(1, 16):
            lp_copy(k).start()
        for k in range(1, 8):
            wp_copy(k).start()
        yield
        total_l = lp_ref[r]
        for k in range(1, 16):
            lp_copy(k).wait_recv()
        for k in range(1, 16):
            total_l = total_l + lp_in[lax.rem(r + 16 - k, 16)]
        total_w = wp_ref[c]
        for k in range(1, 8):
            wp_copy(k).wait_recv()
        for k in range(1, 8):
            total_w = total_w + wp_in[lax.rem(c + 8 - k, 8)]
        piece[pl.ds(0, 24), :] = total_l
        piece[pl.ds(24, 24), :] = total_w
        own_p = pltpu.make_async_copy(piece, p_ref.at[core, y, x, z], local_sems.at[2])
        own_p.start()
        for half in range(2):
            pz.start(half, lambda h: piece.at[pl.ds(h * 24, 24), :])
        yield
        pz.forward()
        yield
        def slot(part, y_of, i):
            return p_ref.at[core, y_of, spots[i], :, pl.ds(part * 24, 24), :]

        def go(part, i):
            ref, key = slot(part, y, i), 48 + 12 * part + 3 * i
            swap(ref, ref, key, near)
            swap(ref, ref, key + 1, across)

        def onward(part, i):
            ref, key = slot(part, yh * 2 + 1 - yl, i), 48 + 12 * part + 3 * i
            arrived(ref, key)
            swap(ref, ref, key + 2, across)

        def both(core_of, part, i):
            return p_ref.at[core_of, pl.ds(0, 4), spots[i], :, pl.ds(part * 24, 24), :]

        def share(part, i):
            key = 48 + 12 * part + 3 * i
            arrived(slot(part, lax.rem(y + 3 + 2 * yl, 4), i), key + 1)
            arrived(slot(part, lax.rem(y + 2, 4), i), key + 2)
            swap(both(core, part, i), both(core, part, i), 72 + 4 * part + i, other)

        own_p.wait()
        pz.finish_near()
        pz.finish_far()
        for half in range(2):
            px.start(half)
        go(1, 0)
        yield
        px.forward()
        yield
        px.finish_near()
        go(1, 1)
        go(1, 2)
        onward(1, 0)
        yield
        px.finish_far()
        go(1, 3)
        onward(1, 1)
        onward(1, 2)
        for i in range(4):
            go(0, i)
        yield
        share(1, 0)
        onward(1, 3)
        onward(0, 0)
        yield
        share(1, 1)
        share(1, 2)
        onward(0, 1)
        onward(0, 2)
        yield
        share(1, 3)
        onward(0, 3)
        share(0, 0)
        yield
        for i in range(4):
            arrived(both(1 - core, 1, i), 76 + i)
        place(1)
        yield
        for i in range(1, 4):
            share(0, i)
        yield
        for i in range(4):
            arrived(both(1 - core, 0, i), 72 + i)
        place(0)
        yield

    def place(part):
        @pl.loop(0, 32)
        def _(i):
            x_of, yh_of, z_of = i // 8, lax.rem(i // 4, 2), lax.rem(i, 4)
            for core_of in range(2):
                for yl_of in range(2):
                    block = p_ref[
                        core_of, yh_of * 2 + yl_of, x_of, z_of, part * 24 : part * 24 + 24, :
                    ]
                    if part == 0:
                        at_k = (z_of * 2 + yl_of) * 192 + (x_of * 2 + yh_of) * 24
                        lanes = pl.ds(core_of * PANEL, PANEL)
                        lkt[pl.ds(pl.multiple_of(at_k, 24), 24), lanes] = block
                    else:
                        at_k = ((x_of * 2 + yh_of) * 2 + core_of) * 96 + z_of * 24
                        lanes = pl.ds(yl_of * PANEL, PANEL)
                        wk[pl.ds(pl.multiple_of(at_k, 24), 24), lanes] = block

    first, second = pl.ds(0, PANEL), pl.ds(PANEL, PANEL)

    def flow_c():
        for n, step in enumerate((0, -1, 1, 2)):
            at_k = pl.ds(pl.multiple_of(l_rings[0].pos(step) * 384, 384), 384)
            for half in (first, second):
                part = COUPLING * dot3((lh[:, at_k], ll[:, at_k]), split(wk[at_k, half]))
                if n == 0:
                    cc[:, half] = part
                else:
                    cc[:, half] += part
            yield

    def flow_chain():
        mids[...] = jnp.zeros_like(mids)

        @pl.loop(0, 6)
        def _(k):
            at_k = pl.ds(pl.multiple_of(k * PANEL, PANEL), PANEL)
            mids[...] += COUPLING * dot3(split(lkt[at_k, :].T), split(wk[at_k, :]))

        def screened(block, s):
            places = lax.broadcasted_iota(jnp.int32, (80, PANEL), 0)
            chosen = jnp.where(places == index_ref[s : s + 1, :], screen_ref[...], 0.0)
            return block + unit() * jnp.sum(chosen, axis=0, keepdims=True)

        inv1 = split(newton_inverse(screened(mids[first, first], 0)))
        x12 = split(mids[first, second])
        b1 = split(dot3(split(mids[second, first]), inv1))
        inv2 = split(newton_inverse(screened(mids[second, second] - dot3(b1, x12), 1)))
        yield

        @pl.loop(0, 5)
        def _(m):
            at_m = pl.ds(pl.multiple_of(m * PANEL, PANEL), PANEL)
            mask1 = 1.0 - hit(0, r * 5 + m)
            mask2 = mask1 * (1.0 - hit(1, r * 5 + m))
            low1 = dot3(split(cc[at_m, first]), inv1) * mask1
            low2 = cc[at_m, second] - dot3(split(low1), x12)
            low2 = dot3(split(low2), inv2) * mask2
            lower[at_m, first] = low1
            lower[at_m, second] = low2
            pair = split(low2)
            eh[at_m, second], el[at_m, second] = pair
            eh[at_m, first], el[at_m, first] = split(low1 - dot3(pair, b1))

        put_lower.start()

        @pl.loop(0, 6)
        def _(k):
            at_k = pl.ds(pl.multiple_of(k * PANEL, PANEL), PANEL)
            panel = split(lkt[at_k, :])
            now = lh[:, at_k].astype(F32) + ll[:, at_k].astype(F32)
            now = now - dot3((eh[...], el[...]), panel, ((1,), (1,)))
            lh[:, at_k], ll[:, at_k] = split(now)
            for put in put_left(k):
                put.start()

        yield

    def put_left(k):
        at_k = pl.ds(pl.multiple_of(k * PANEL, PANEL), PANEL)
        return (
            pltpu.make_async_copy(lh.at[:, at_k], high_ref.at[:, at_k], left_sems.at[0, k]),
            pltpu.make_async_copy(ll.at[:, at_k], low_ref.at[:, at_k], left_sems.at[1, k]),
        )

    put_lower = pltpu.make_async_copy(lower, lower_ref, local_sems.at[4])

    makers = {
        "w0": flow_w0, "wy": flow_wy, "w1": flow_w1, "l0": flow_l0, "ly": flow_ly,
        "l1": flow_l1, "p": flow_p, "t": flow_t, "c": flow_c, "chain": flow_chain,
    }
    flows = {}
    for name in SCHEDULE:
        if name not in flows:
            flows[name] = makers[name]()
        next(flows[name])
    for flow in flows.values():
        for _ in flow:
            pass

    ring = w_rings[0]
    from_other(x, yh, 28)
    from_other(x, 1 - yh, 29)
    from_other(ring.pos(-1), yh, 30)
    from_other(ring.pos(1), yh, 31)
    from_other(ring.pos(2), yh, 32)
    from_other(ring.pos(-1), 1 - yh, 33)
    from_other(ring.pos(1), 1 - yh, 34)
    from_other(ring.pos(2), 1 - yh, 35)
    put_w.wait()
    put_lower.wait()
    for k in range(6):
        for put in put_left(k):
            put.wait()
    for k in range(1, 16):
        lp_copy(k).wait_send()
    for k in range(1, 8):
        wp_copy(k).wait_send()
    for ring in w_rings + l_rings + [pz, px]:
        ring.drain()
    for copy in swaps:
        copy.wait_send()


def gather(left_t, right, index, screen):
    any_spec = pl.BlockSpec(memory_space=pl.ANY)
    vmem_spec = pl.BlockSpec(memory_space=pltpu.VMEM)
    dma = pltpu.SemaphoreType.DMA
    return pl.pallas_call(
        gather_kernel,
        out_shape=(
            jax.ShapeDtypeStruct((16, 96, 2560), F32),
            jax.ShapeDtypeStruct((1280, 1536), BF),
            jax.ShapeDtypeStruct((1280, 1536), BF),
            jax.ShapeDtypeStruct((1280, 512), F32),
        ),
        in_specs=[any_spec, any_spec, vmem_spec, vmem_spec],
        out_specs=(any_spec, any_spec, any_spec, any_spec),
        scratch_shapes=[
            pltpu.VMEM((1536, 1280), F32),
            pltpu.VMEM((2, 4, 4, 4, 48, PANEL), F32),
            pltpu.VMEM((1536, 512), F32),
            pltpu.VMEM((1536, 512), F32),
            pltpu.VMEM((1280, 1536), BF),
            pltpu.VMEM((1280, 1536), BF),
            pltpu.VMEM((1280, 512), F32),
            pltpu.VMEM((1280, 512), F32),
            pltpu.VMEM((1280, 512), BF),
            pltpu.VMEM((1280, 512), BF),
            pltpu.VMEM((512, 512), F32),
            pltpu.VMEM((16, 24, PANEL), F32),
            pltpu.VMEM((8, 24, PANEL), F32),
            pltpu.VMEM((16, 24, PANEL), F32),
            pltpu.VMEM((8, 24, PANEL), F32),
            pltpu.VMEM((48, PANEL), F32),
            pltpu.VMEM((192, 1280), F32),
            pltpu.VMEM((96, 2560), F32),
            dma((80,)),
            dma((80,)),
            dma((16,)),
            dma((16,)),
            dma((8,)),
            dma((8,)),
            dma((6,)),
            dma((2, 6)),
        ],
        compiler_params=pltpu.CompilerParams(
            collective_id=0, has_side_effects=True, vmem_limit_bytes=58 << 20
        ),
        name="exchange",
    )(left_t, right, index, screen)


def product_kernel(index_ref, lh_ref, ll_ref, w_ref, lower_ref, screen_ref, o_ref):
    n = pl.program_id(0)
    w = split(w_ref[...])
    o_ref[...] = COUPLING * dot3((lh_ref[...], ll_ref[...]), w)
    row0 = lax.axis_index("row") * 5
    block = lax.axis_index("col") * 10 + n
    rel = block - row0

    @pl.when((rel >= 0) & (rel < 5))
    def _():
        at = pl.ds(pl.multiple_of(rel * PANEL, PANEL), PANEL)
        o_ref[at, :] += unit() * screen_ref[pl.ds(block, 1), :]

    for s in range(2):

        @pl.when(block == index_ref[s])
        def _():
            for m in range(5):
                hit = row0 + m == index_ref[0]
                if s == 1:
                    hit = hit | (row0 + m == index_ref[1])

                @pl.when(jnp.logical_not(hit))
                def _():
                    at = pl.ds(m * PANEL, PANEL)
                    o_ref[at, :] = lower_ref[at, s * PANEL : (s + 1) * PANEL]


def product(index, lh, ll, w, lower, screen):
    once = dict(pipeline_mode=pl.Buffered(1))
    return pl.pallas_call(
        product_kernel,
        out_shape=jax.ShapeDtypeStruct((1280, 2560), F32),
        grid_spec=pltpu.PrefetchScalarGridSpec(
            num_scalar_prefetch=1,
            grid=(10,),
            in_specs=[
                pl.BlockSpec((1280, 1536), lambda n, s: (0, 0), **once),
                pl.BlockSpec((1280, 1536), lambda n, s: (0, 0), **once),
                pl.BlockSpec((1536, PANEL), lambda n, s: (0, n)),
                pl.BlockSpec((1280, 512), lambda n, s: (0, 0), **once),
                pl.BlockSpec((80, PANEL), lambda n, s: (0, 0), **once),
            ],
            out_specs=pl.BlockSpec((1280, PANEL), lambda n, s: (0, n)),
        ),
        compiler_params=pltpu.CompilerParams(vmem_limit_bytes=56 << 20),
        name="product",
    )(index, lh, ll, w, lower, screen)


def shards(left_pairs, right_pairs, pair_weight, screen, panel_index):
    weighted = right_pairs * pair_weight[:, None]
    screen = screen.reshape(80, PANEL)
    index = jnp.broadcast_to(panel_index[:, None], (SECTIONS, PANEL))
    w_all, lh, ll, lower = gather(left_pairs.T, weighted, index, screen)
    return product(panel_index, lh, ll, w_all.reshape(1536, 2560), lower, screen)


def solution(mesh):
    return jax.shard_map(
        shards,
        mesh=mesh,
        in_specs=(P("row", "col"), P("row", "col"), P("row"), P(), P()),
        out_specs=P("row", "col"),
        check_vma=False,
    )
```

```python
import jax
import jax.numpy as jnp
from jax import lax
from jax.experimental import pallas as pl
from jax.experimental.pallas import tpu as pltpu
from jax.sharding import PartitionSpec as P

PANEL = 256
SECTIONS = 2
NS_STEPS = 3

COUPLING = 0.08

SCHEDULE = (
    "p", "wy", "ly", "w0", "l0", "p", "p", "p", "wy", "ly",
    "w0", "l0", "p", "w0", "l0", "w1", "l1", "p", "w1", "l1",
    "p", "p", "p", "w0", "p", "w0", "w1", "l1", "p", "t",
    "chain", "w1", "w1", "t", "chain",
)

MESH = pl.DeviceIdType.MESH
F32 = jnp.float32
BF = jnp.bfloat16


def remote(src, dst, send_sem, recv_sem, target):
    return pltpu.make_async_remote_copy(
        src_ref=src,
        dst_ref=dst,
        send_sem=send_sem,
        recv_sem=recv_sem,
        device_id=target,
        device_id_type=MESH,
    )


class Ring:
    def __init__(self, ref, me, ahead, behind, send_sems, recv_sems, base):
        self.ref, self.me = ref, me
        self.ahead, self.behind = ahead, behind
        self.send_sems, self.recv_sems, self.base = send_sems, recv_sems, base
        self.sent = []

    def pos(self, step):
        return lax.rem(self.me + 4 + step, 4)

    def send(self, src, pos, half, key, target):
        copy = remote(
            src,
            self.ref(pos, half),
            self.send_sems.at[self.base + key],
            self.recv_sems.at[self.base + key],
            target,
        )
        copy.start()
        self.sent.append(copy)

    def arrived(self, pos, half, key):
        ref = self.ref(pos, half)
        remote(
            ref,
            ref,
            self.send_sems.at[self.base + key],
            self.recv_sems.at[self.base + key],
            self.ahead,
        ).wait_recv()

    def start(self, half_at, source=None):
        source = source or (lambda half: self.ref(self.me, half))
        first, second = (0, 1) if half_at == 0 else (1, 0)
        self.send(source(first), self.me, first, first, self.ahead)
        self.send(source(second), self.me, second, 2 + second, self.behind)

    def forward(self):
        self.arrived(self.pos(-1), 0, 0)
        self.send(self.ref(self.pos(-1), 0), self.pos(-1), 0, 4, self.ahead)
        self.arrived(self.pos(1), 1, 3)
        self.send(self.ref(self.pos(1), 1), self.pos(1), 1, 5, self.behind)

    def finish_near(self):
        self.arrived(self.pos(-1), 1, 1)
        self.arrived(self.pos(1), 0, 2)

    def finish_far(self):
        self.arrived(self.pos(2), 0, 4)
        self.arrived(self.pos(2), 1, 5)

    def drain(self):
        for copy in self.sent:
            copy.wait_send()


def split(a):
    hi = a.astype(BF)
    return hi, (a - hi.astype(F32)).astype(BF)


def dot3(a, b, dims=((1,), (0,))):
    def one(p, q):
        return lax.dot_general(p, q, (dims, ((), ())), preferred_element_type=F32)

    return one(a[0], b[0]) + one(a[0], b[1]) + one(a[1], b[0])


def unit():
    rows = lax.broadcasted_iota(jnp.int32, (PANEL, PANEL), 0)
    cols = lax.broadcasted_iota(jnp.int32, (PANEL, PANEL), 1)
    return (rows == cols).astype(F32)


def newton_inverse(matrix_in):
    eye = unit()
    approx = eye / jnp.sum(matrix_in * eye, axis=0, keepdims=True)
    whole = split(matrix_in)
    for _ in range(NS_STEPS):
        now = split(approx)
        product = dot3(whole, now)
        approx = dot3(now, split(2.0 * eye - product))
    return approx


def gather_kernel(
    left_ref,
    right_ref,
    weight_ref,
    index_ref,
    screen_ref,
    w_ref,
    high_ref,
    low_ref,
    lower_ref,
    lt,
    p_ref,
    lkt,
    wk,
    lh,
    ll,
    cc,
    lower,
    eh,
    el,
    mids,
    lp_ref,
    wp_ref,
    lp_in,
    wp_in,
    piece,
    own_left,
    own_right,
    send_sems,
    recv_sems,
    lps_sems,
    lpr_sems,
    wps_sems,
    wpr_sems,
    local_sems,
    left_sems,
):
    r = lax.axis_index("row")
    c = lax.axis_index("col")
    core = lax.rem(r, 2)
    yh = lax.rem(r // 2, 2)
    x = r // 4
    yl = lax.rem(c, 2)
    z = c // 2
    y = yh * 2 + yl

    def at(x=x, y=y, z=z, core=core):
        return {"row": (x * 2 + y // 2) * 2 + core, "col": z * 2 + lax.rem(y, 2)}

    x_up, x_down = at(x=lax.rem(x + 1, 4)), at(x=lax.rem(x + 3, 4))
    z_up, z_down = at(z=lax.rem(z + 1, 4)), at(z=lax.rem(z + 3, 4))
    far = at(y=lax.rem(y + 2, 4))
    near = at(y=yh * 2 + 1 - yl)
    other = at(core=1 - core)

    def l_slot(slot, half):
        return lt.at[pl.ds(pl.multiple_of(slot * 192 + half * 96, 96), 96), :]

    own_l = pltpu.make_async_copy(left_ref, own_left, local_sems.at[0])
    own_w = pltpu.make_async_copy(right_ref, own_right, local_sems.at[1])
    own_l.start()
    own_w.start()
    put_w = pltpu.make_async_copy(own_right, w_ref.at[r], local_sems.at[3])
    put_l = pltpu.make_async_copy(
        own_left, lt.at[pl.ds(pl.multiple_of(c * 192, 192), 192), :], local_sems.at[5]
    )

    barrier = pltpu.get_barrier_semaphore()

    def greet_row(k, carry):
        pl.semaphore_signal(
            barrier, 1, device_id={"row": lax.rem(r + k, 16), "col": c}, device_id_type=MESH
        )
        return carry

    def greet_col(k, carry):
        pl.semaphore_signal(
            barrier, 1, device_id={"row": r, "col": lax.rem(c + k, 8)}, device_id_type=MESH
        )
        return carry

    lax.fori_loop(1, 16, greet_row, 0)
    lax.fori_loop(1, 8, greet_col, 0)
    across = at(y=lax.rem(y + 3 + 2 * yl, 4))
    pl.semaphore_signal(barrier, 1, device_id=across, device_id_type=MESH)

    def hit(s, block):
        return jnp.where(index_ref[:, s : s + 1] == block, 1.0, 0.0)

    own_l.wait()
    own_w.wait()
    square = lax.broadcasted_iota(jnp.int32, (96, 96), 0) == lax.broadcasted_iota(
        jnp.int32, (96, 96), 1
    )
    weights = jnp.sum(jnp.where(square, weight_ref[...], 0.0), axis=1, keepdims=True)
    own_right[...] = own_right[...] * weights
    put_l.start()
    put_w.start()
    for s in range(SECTIONS):
        part = jnp.zeros((192, PANEL), F32)
        for b in range(5):
            part = part + own_left[:, b * PANEL : (b + 1) * PANEL] * hit(s, r * 5 + b)
        for g in range(8):
            lp_ref[g * 2 + s] = part[g * 24 : g * 24 + 24]
        part = jnp.zeros((96, PANEL), F32)
        for b in range(10):
            part = part + own_right[:, b * PANEL : (b + 1) * PANEL] * hit(s, c * 10 + b)
        for g in range(4):
            wp_ref[g * 2 + s] = part[g * 24 : g * 24 + 24]
    pl.semaphore_wait(barrier, 23)

    def lp_copy(k):
        to = lax.rem(r + k, 16)
        return remote(
            lp_ref.at[to], lp_in.at[r], lps_sems.at[k], lpr_sems.at[k], {"row": to, "col": c}
        )

    def wp_copy(k):
        to = lax.rem(c + k, 8)
        return remote(
            wp_ref.at[to], wp_in.at[c], wps_sems.at[k], wpr_sems.at[k], {"row": r, "col": to}
        )

    def w_place(yh_of):
        return lambda pos, half: w_ref.at[(pos * 2 + yh_of) * 2 + core, pl.ds(half * 48, 48), :]

    def l_place(yl_of):
        return lambda pos, half: l_slot(pos * 2 + yl_of, half)

    w_rings = [
        Ring(w_place(yh), x, x_up, x_down, send_sems, recv_sems, 0),
        Ring(w_place(1 - yh), x, x_up, x_down, send_sems, recv_sems, 6),
    ]
    l_rings = [
        Ring(l_place(yl), z, z_up, z_down, send_sems, recv_sems, 12),
        Ring(l_place(1 - yl), z, z_up, z_down, send_sems, recv_sems, 18),
    ]
    pz = Ring(
        lambda pos, half: p_ref.at[core, y, x, pos, pl.ds(half * 24, 24), :],
        z, z_up, z_down, send_sems, recv_sems, 36,
    )
    px = Ring(
        lambda pos, half: p_ref.at[core, y, pos, pl.ds(half * 2, 2)],
        x, x_up, x_down, send_sems, recv_sems, 42,
    )
    spots = [x, px.pos(-1), px.pos(1), px.pos(2)]

    def w_own(half):
        return own_right.at[pl.ds(half * 48, 48), :]

    def l_own(half):
        return left_ref.at[pl.ds(half * 96, 96), :]

    swaps = []

    def swap(src, dst, key, target):
        copy = remote(src, dst, send_sems.at[key], recv_sems.at[key], target)
        copy.start()
        swaps.append(copy)

    def to_other(pos, yh_of, key):
        slot = w_ref.at[(pos * 2 + yh_of) * 2 + core]
        swap(slot, slot, key, other)

    def arrived(ref, key):
        remote(ref, ref, send_sems.at[key], recv_sems.at[key], other).wait_recv()

    def from_other(pos, yh_of, key):
        arrived(w_ref.at[(pos * 2 + yh_of) * 2 + 1 - core], key)

    def flow_w0():
        ring = w_rings[0]
        ring.start(0, w_own)
        yield
        ring.start(1, w_own)
        yield
        swap(own_right, w_ref.at[r], 28, other)
        ring.forward()
        yield
        ring.finish_near()
        to_other(ring.pos(-1), yh, 30)
        to_other(ring.pos(1), yh, 31)
        yield
        ring.finish_far()
        to_other(ring.pos(2), yh, 32)
        yield

    def flow_wy():
        for half in range(2):
            swap(w_own(half), w_place(yh)(x, half), 24 + half, far)
            yield

    def follow(ring, place, me, key):
        for half in range(2):
            ref = place(me, half)
            arrived(ref, key + half)
            ring.send(ref, me, half, half, ring.ahead)
            ring.send(ref, me, half, 2 + half, ring.behind)
            yield

    def flow_w1():
        ring = w_rings[1]
        yield from follow(ring, w_place(1 - yh), x, 24)
        to_other(x, 1 - yh, 29)
        ring.forward()
        yield
        ring.finish_near()
        to_other(ring.pos(-1), 1 - yh, 33)
        to_other(ring.pos(1), 1 - yh, 34)
        yield
        ring.finish_far()
        to_other(ring.pos(2), 1 - yh, 35)
        yield

    def flow_l0():
        ring = l_rings[0]
        ring.start(0, l_own)
        yield
        ring.start(1, l_own)
        yield
        ring.forward()
        yield

    def flow_ly():
        for half in range(2):
            swap(l_own(half), l_place(yl)(z, half), 26 + half, near)
            yield

    def flow_l1():
        ring = l_rings[1]
        yield from follow(ring, l_place(1 - yl), z, 26)
        ring.forward()
        yield

    def turn(pos):
        at_k = pl.ds(pl.multiple_of(pos * 384, 384), 384)

        @pl.loop(0, 5)
        def _(m):
            at_m = pl.ds(pl.multiple_of(m * PANEL, PANEL), PANEL)
            hi, lo = split(lt[at_k, at_m].T)
            lh[at_m, at_k] = hi
            ll[at_m, at_k] = lo

    def flow_t():
        put_l.wait()
        for ring in l_rings:
            ring.finish_near()
        for step in (0, -1, 1):
            turn(l_rings[0].pos(step))
        yield
        for ring in l_rings:
            ring.finish_far()
        turn(l_rings[0].pos(2))
        yield

    def flow_p():
        for k in range(1, 16):
            lp_copy(k).start()
        for k in range(1, 8):
            wp_copy(k).start()
        yield
        total_l = lp_ref[r]
        for k in range(1, 16):
            lp_copy(k).wait_recv()
        for k in range(1, 16):
            total_l = total_l + lp_in[lax.rem(r + 16 - k, 16)]
        total_w = wp_ref[c]
        for k in range(1, 8):
            wp_copy(k).wait_recv()
        for k in range(1, 8):
            total_w = total_w + wp_in[lax.rem(c + 8 - k, 8)]
        piece[pl.ds(0, 24), :] = total_l
        piece[pl.ds(24, 24), :] = total_w
        own_p = pltpu.make_async_copy(piece, p_ref.at[core, y, x, z], local_sems.at[2])
        own_p.start()
        for half in range(2):
            pz.start(half, lambda h: piece.at[pl.ds(h * 24, 24), :])
        yield
        pz.forward()
        yield
        def slot(y_of, i):
            return p_ref.at[core, y_of, spots[i]]

        def go(i):
            swap(slot(y, i), slot(y, i), 55 + 3 * i, near)
            swap(slot(y, i), slot(y, i), 56 + 3 * i, across)

        def onward(i):
            ref = slot(yh * 2 + 1 - yl, i)
            arrived(ref, 55 + 3 * i)
            swap(ref, ref, 57 + 3 * i, across)

        def share(i):
            arrived(slot(lax.rem(y + 3 + 2 * yl, 4), i), 56 + 3 * i)
            arrived(slot(lax.rem(y + 2, 4), i), 57 + 3 * i)
            whole = p_ref.at[core, pl.ds(0, 4), spots[i]]
            swap(whole, whole, 67 + i, other)

        own_p.wait()
        pz.finish_near()
        pz.finish_far()
        for half in range(2):
            px.start(half)
        go(0)
        yield
        px.forward()
        yield
        px.finish_near()
        go(1)
        go(2)
        onward(0)
        yield
        px.finish_far()
        go(3)
        onward(1)
        onward(2)
        yield
        share(0)
        onward(3)
        yield
        share(1)
        share(2)
        yield
        share(3)
        yield
        for i in range(4):
            arrived(p_ref.at[1 - core, pl.ds(0, 4), spots[i]], 67 + i)
        place_panels()
        yield

    def place_panels():
        @pl.loop(0, 32)
        def _(i):
            x_of, yh_of, z_of = i // 8, lax.rem(i // 4, 2), lax.rem(i, 4)
            for core_of in range(2):
                for yl_of in range(2):
                    block = p_ref[core_of, yh_of * 2 + yl_of, x_of, z_of]
                    at_l = pl.multiple_of((z_of * 2 + yl_of) * 192 + (x_of * 2 + yh_of) * 24, 24)
                    at_w = pl.multiple_of(
                        ((x_of * 2 + yh_of) * 2 + core_of) * 96 + z_of * 24, 24
                    )
                    lkt[pl.ds(at_l, 24), pl.ds(core_of * PANEL, PANEL)] = block[:24]
                    wk[pl.ds(at_w, 24), pl.ds(yl_of * PANEL, PANEL)] = block[24:]

    first, second = pl.ds(0, PANEL), pl.ds(PANEL, PANEL)

    def flow_chain():
        mids[...] = jnp.zeros_like(mids)

        @pl.loop(0, 6)
        def _(k):
            at_k = pl.ds(pl.multiple_of(k * PANEL, PANEL), PANEL)
            mids[...] += COUPLING * dot3(split(lkt[at_k, :].T), split(wk[at_k, :]))

        def screened(block, s):
            places = lax.broadcasted_iota(jnp.int32, (80, PANEL), 0)
            chosen = jnp.where(places == index_ref[:, s : s + 1], screen_ref[...], 0.0)
            return block + unit() * jnp.sum(chosen, axis=0, keepdims=True)

        inv1 = split(newton_inverse(screened(mids[first, first], 0)))
        x12 = split(mids[first, second])
        b1 = split(dot3(split(mids[second, first]), inv1))
        inv2 = split(newton_inverse(screened(mids[second, second] - dot3(b1, x12), 1)))
        yield
        for half in (first, second):
            cc[:, half] = COUPLING * dot3((lh[...], ll[...]), split(wk[:, half]))

        @pl.loop(0, 5)
        def _(m):
            at_m = pl.ds(pl.multiple_of(m * PANEL, PANEL), PANEL)
            mask1 = 1.0 - hit(0, r * 5 + m)
            mask2 = mask1 * (1.0 - hit(1, r * 5 + m))
            low1 = dot3(split(cc[at_m, first]), inv1) * mask1
            low2 = cc[at_m, second] - dot3(split(low1), x12)
            low2 = dot3(split(low2), inv2) * mask2
            lower[at_m, first] = low1
            lower[at_m, second] = low2
            pair = split(low2)
            eh[at_m, second], el[at_m, second] = pair
            eh[at_m, first], el[at_m, first] = split(low1 - dot3(pair, b1))

        put_lower.start()

        @pl.loop(0, 6)
        def _(k):
            at_k = pl.ds(pl.multiple_of(k * PANEL, PANEL), PANEL)
            panel = split(lkt[at_k, :])
            now = lh[:, at_k].astype(F32) + ll[:, at_k].astype(F32)
            now = now - dot3((eh[...], el[...]), panel, ((1,), (1,)))
            lh[:, at_k], ll[:, at_k] = split(now)
            for put in put_left(k):
                put.start()

        yield

    def put_left(k):
        at_k = pl.ds(pl.multiple_of(k * PANEL, PANEL), PANEL)
        return (
            pltpu.make_async_copy(lh.at[:, at_k], high_ref.at[:, at_k], left_sems.at[0, k]),
            pltpu.make_async_copy(ll.at[:, at_k], low_ref.at[:, at_k], left_sems.at[1, k]),
        )

    put_lower = pltpu.make_async_copy(lower, lower_ref, local_sems.at[4])

    makers = {
        "w0": flow_w0, "wy": flow_wy, "w1": flow_w1, "l0": flow_l0, "ly": flow_ly,
        "l1": flow_l1, "p": flow_p, "t": flow_t, "chain": flow_chain,
    }
    flows = {}
    for name in SCHEDULE:
        if name not in flows:
            flows[name] = makers[name]()
        next(flows[name])
    for flow in flows.values():
        for _ in flow:
            pass

    ring = w_rings[0]
    from_other(x, yh, 28)
    from_other(x, 1 - yh, 29)
    from_other(ring.pos(-1), yh, 30)
    from_other(ring.pos(1), yh, 31)
    from_other(ring.pos(2), yh, 32)
    from_other(ring.pos(-1), 1 - yh, 33)
    from_other(ring.pos(1), 1 - yh, 34)
    from_other(ring.pos(2), 1 - yh, 35)
    put_w.wait()
    put_lower.wait()
    for k in range(6):
        for put in put_left(k):
            put.wait()
    for k in range(1, 16):
        lp_copy(k).wait_send()
    for k in range(1, 8):
        wp_copy(k).wait_send()
    for ring in w_rings + l_rings + [pz, px]:
        ring.drain()
    for copy in swaps:
        copy.wait_send()


def gather(left_t, right, weight, index, screen):
    any_spec = pl.BlockSpec(memory_space=pl.ANY)
    vmem_spec = pl.BlockSpec(memory_space=pltpu.VMEM)
    dma = pltpu.SemaphoreType.DMA
    return pl.pallas_call(
        gather_kernel,
        out_shape=(
            jax.ShapeDtypeStruct((16, 96, 2560), F32),
            jax.ShapeDtypeStruct((1280, 1536), BF),
            jax.ShapeDtypeStruct((1280, 1536), BF),
            jax.ShapeDtypeStruct((1280, 512), F32),
        ),
        in_specs=[any_spec, any_spec, vmem_spec, vmem_spec, vmem_spec],
        out_specs=(any_spec, any_spec, any_spec, any_spec),
        scratch_shapes=[
            pltpu.VMEM((1536, 1280), F32),
            pltpu.VMEM((2, 4, 4, 4, 48, PANEL), F32),
            pltpu.VMEM((1536, 512), F32),
            pltpu.VMEM((1536, 512), F32),
            pltpu.VMEM((1280, 1536), BF),
            pltpu.VMEM((1280, 1536), BF),
            pltpu.VMEM((1280, 512), F32),
            pltpu.VMEM((1280, 512), F32),
            pltpu.VMEM((1280, 512), BF),
            pltpu.VMEM((1280, 512), BF),
            pltpu.VMEM((512, 512), F32),
            pltpu.VMEM((16, 24, PANEL), F32),
            pltpu.VMEM((8, 24, PANEL), F32),
            pltpu.VMEM((16, 24, PANEL), F32),
            pltpu.VMEM((8, 24, PANEL), F32),
            pltpu.VMEM((48, PANEL), F32),
            pltpu.VMEM((192, 1280), F32),
            pltpu.VMEM((96, 2560), F32),
            dma((71,)),
            dma((71,)),
            dma((16,)),
            dma((16,)),
            dma((8,)),
            dma((8,)),
            dma((6,)),
            dma((2, 6)),
        ],
        compiler_params=pltpu.CompilerParams(
            collective_id=0, has_side_effects=True, vmem_limit_bytes=58 << 20
        ),
        name="exchange",
    )(left_t, right, weight, index, screen)


def product_kernel(index_ref, lh_ref, ll_ref, w_ref, lower_ref, screen_ref, o_ref):
    n = pl.program_id(0)
    w = split(w_ref[...])
    o_ref[...] = COUPLING * dot3((lh_ref[...], ll_ref[...]), w)
    row0 = lax.axis_index("row") * 5
    block = lax.axis_index("col") * 10 + n
    rel = block - row0

    @pl.when((rel >= 0) & (rel < 5))
    def _():
        at = pl.ds(pl.multiple_of(rel * PANEL, PANEL), PANEL)
        o_ref[at, :] += unit() * screen_ref[pl.ds(block, 1), :]

    for s in range(2):

        @pl.when(block == index_ref[s])
        def _():
            for m in range(5):
                hit = row0 + m == index_ref[0]
                if s == 1:
                    hit = hit | (row0 + m == index_ref[1])

                @pl.when(jnp.logical_not(hit))
                def _():
                    at = pl.ds(m * PANEL, PANEL)
                    o_ref[at, :] = lower_ref[at, s * PANEL : (s + 1) * PANEL]


def product(index, lh, ll, w, lower, screen):
    once = dict(pipeline_mode=pl.Buffered(1))
    return pl.pallas_call(
        product_kernel,
        out_shape=jax.ShapeDtypeStruct((1280, 2560), F32),
        grid_spec=pltpu.PrefetchScalarGridSpec(
            num_scalar_prefetch=1,
            grid=(10,),
            in_specs=[
                pl.BlockSpec((1280, 1536), lambda n, s: (0, 0), **once),
                pl.BlockSpec((1280, 1536), lambda n, s: (0, 0), **once),
                pl.BlockSpec((1536, PANEL), lambda n, s: (0, n)),
                pl.BlockSpec((1280, 512), lambda n, s: (0, 0), **once),
                pl.BlockSpec((80, PANEL), lambda n, s: (0, 0), **once),
            ],
            out_specs=pl.BlockSpec((1280, PANEL), lambda n, s: (0, n)),
        ),
        compiler_params=pltpu.CompilerParams(vmem_limit_bytes=56 << 20),
        name="product",
    )(index, lh, ll, w, lower, screen)


def shards(left_pairs, right_pairs, pair_weight, screen, panel_index):
    screen = screen.reshape(80, PANEL)
    w_all, lh, ll, lower = gather(
        left_pairs.T,
        right_pairs,
        pair_weight.reshape(1, 96),
        panel_index.reshape(1, SECTIONS),
        screen,
    )
    return product(panel_index, lh, ll, w_all.reshape(1536, 2560), lower, screen)


def solution(mesh):
    return jax.shard_map(
        shards,
        mesh=mesh,
        in_specs=(P("row", "col"), P("row", "col"), P("row"), P(), P()),
        out_specs=P("row", "col"),
        check_vma=False,
    )
```

```python
import jax
import jax.numpy as jnp
from jax import lax
from jax.experimental import pallas as pl
from jax.experimental.pallas import tpu as pltpu
from jax.sharding import PartitionSpec as P

PANEL = 256
SECTIONS = 2
NS_STEPS = 3

COUPLING = 0.08

SCHEDULE = (
    "p", "wy", "ly", "w0", "l0", "p", "p", "p", "wy", "ly",
    "w0", "l0", "p", "w0", "l0", "w1", "l1", "p", "w1", "l1",
    "p", "p", "p", "w0", "p", "w0", "w1", "l1", "t", "p",
    "chain", "w1", "w1", "t", "chain",
)

MESH = pl.DeviceIdType.MESH
F32 = jnp.float32
BF = jnp.bfloat16


def remote(src, dst, send_sem, recv_sem, target):
    return pltpu.make_async_remote_copy(
        src_ref=src,
        dst_ref=dst,
        send_sem=send_sem,
        recv_sem=recv_sem,
        device_id=target,
        device_id_type=MESH,
    )


class Ring:
    def __init__(self, ref, me, ahead, behind, send_sems, recv_sems, base):
        self.ref, self.me = ref, me
        self.ahead, self.behind = ahead, behind
        self.send_sems, self.recv_sems, self.base = send_sems, recv_sems, base
        self.sent = []

    def pos(self, step):
        return lax.rem(self.me + 4 + step, 4)

    def send(self, src, pos, half, key, target):
        copy = remote(
            src,
            self.ref(pos, half),
            self.send_sems.at[self.base + key],
            self.recv_sems.at[self.base + key],
            target,
        )
        copy.start()
        self.sent.append(copy)

    def arrived(self, pos, half, key):
        ref = self.ref(pos, half)
        remote(
            ref,
            ref,
            self.send_sems.at[self.base + key],
            self.recv_sems.at[self.base + key],
            self.ahead,
        ).wait_recv()

    def start(self, half_at, source=None):
        source = source or (lambda half: self.ref(self.me, half))
        first, second = (0, 1) if half_at == 0 else (1, 0)
        self.send(source(first), self.me, first, first, self.ahead)
        self.send(source(second), self.me, second, 2 + second, self.behind)

    def forward(self):
        self.arrived(self.pos(-1), 0, 0)
        self.send(self.ref(self.pos(-1), 0), self.pos(-1), 0, 4, self.ahead)
        self.arrived(self.pos(1), 1, 3)
        self.send(self.ref(self.pos(1), 1), self.pos(1), 1, 5, self.behind)

    def finish_near(self):
        self.arrived(self.pos(-1), 1, 1)
        self.arrived(self.pos(1), 0, 2)

    def finish_far(self):
        self.arrived(self.pos(2), 0, 4)
        self.arrived(self.pos(2), 1, 5)

    def drain(self):
        for copy in self.sent:
            copy.wait_send()


def split(a):
    hi = a.astype(BF)
    return hi, (a - hi.astype(F32)).astype(BF)


def dot3(a, b, dims=((1,), (0,))):
    def one(p, q):
        return lax.dot_general(p, q, (dims, ((), ())), preferred_element_type=F32)

    return one(a[0], b[0]) + one(a[0], b[1]) + one(a[1], b[0])


def unit():
    rows = lax.broadcasted_iota(jnp.int32, (PANEL, PANEL), 0)
    cols = lax.broadcasted_iota(jnp.int32, (PANEL, PANEL), 1)
    return (rows == cols).astype(F32)


def newton_inverse(matrix_in):
    eye = unit()
    approx = eye / jnp.sum(matrix_in * eye, axis=0, keepdims=True)
    whole = split(matrix_in)
    for _ in range(NS_STEPS):
        now = split(approx)
        product = dot3(whole, now)
        approx = dot3(now, split(2.0 * eye - product))
    return approx


def gather_kernel(
    left_ref,
    right_ref,
    weight_ref,
    index_ref,
    screen_ref,
    w_ref,
    high_ref,
    low_ref,
    lower_ref,
    lt,
    p_ref,
    lkt,
    wk,
    lh,
    ll,
    cc,
    lower,
    eh,
    el,
    mids,
    lp_ref,
    wp_ref,
    lp_in,
    wp_in,
    piece,
    own_left,
    own_right,
    send_sems,
    recv_sems,
    lps_sems,
    lpr_sems,
    wps_sems,
    wpr_sems,
    local_sems,
    left_sems,
):
    r = lax.axis_index("row")
    c = lax.axis_index("col")
    core = lax.rem(r, 2)
    yh = lax.rem(r // 2, 2)
    x = r // 4
    yl = lax.rem(c, 2)
    z = c // 2
    y = yh * 2 + yl

    def at(x=x, y=y, z=z, core=core):
        return {"row": (x * 2 + y // 2) * 2 + core, "col": z * 2 + lax.rem(y, 2)}

    x_up, x_down = at(x=lax.rem(x + 1, 4)), at(x=lax.rem(x + 3, 4))
    z_up, z_down = at(z=lax.rem(z + 1, 4)), at(z=lax.rem(z + 3, 4))
    far = at(y=lax.rem(y + 2, 4))
    near = at(y=yh * 2 + 1 - yl)
    other = at(core=1 - core)

    def l_slot(slot, half):
        return lt.at[pl.ds(pl.multiple_of(slot * 192 + half * 96, 96), 96), :]

    own_l = pltpu.make_async_copy(left_ref, own_left, local_sems.at[0])
    own_w = pltpu.make_async_copy(right_ref, own_right, local_sems.at[1])
    own_l.start()
    own_w.start()
    put_w = pltpu.make_async_copy(own_right, w_ref.at[r], local_sems.at[3])
    put_l = pltpu.make_async_copy(
        own_left, lt.at[pl.ds(pl.multiple_of(c * 192, 192), 192), :], local_sems.at[5]
    )

    barrier = pltpu.get_barrier_semaphore()

    def greet_row(k, carry):
        pl.semaphore_signal(
            barrier, 1, device_id={"row": lax.rem(r + k, 16), "col": c}, device_id_type=MESH
        )
        return carry

    def greet_col(k, carry):
        pl.semaphore_signal(
            barrier, 1, device_id={"row": r, "col": lax.rem(c + k, 8)}, device_id_type=MESH
        )
        return carry

    lax.fori_loop(1, 16, greet_row, 0)
    lax.fori_loop(1, 8, greet_col, 0)
    across = at(y=lax.rem(y + 3 + 2 * yl, 4))
    pl.semaphore_signal(barrier, 1, device_id=across, device_id_type=MESH)

    def hit(s, block):
        return jnp.where(index_ref[:, s : s + 1] == block, 1.0, 0.0)

    own_l.wait()
    own_w.wait()
    square = lax.broadcasted_iota(jnp.int32, (96, 96), 0) == lax.broadcasted_iota(
        jnp.int32, (96, 96), 1
    )
    weights = jnp.sum(jnp.where(square, weight_ref[...], 0.0), axis=1, keepdims=True)
    own_right[...] = own_right[...] * weights
    put_l.start()
    put_w.start()
    for s in range(SECTIONS):
        part = jnp.zeros((192, PANEL), F32)
        for b in range(5):
            part = part + own_left[:, b * PANEL : (b + 1) * PANEL] * hit(s, r * 5 + b)
        for g in range(8):
            lp_ref[g * 2 + s] = part[g * 24 : g * 24 + 24]
        part = jnp.zeros((96, PANEL), F32)
        for b in range(10):
            part = part + own_right[:, b * PANEL : (b + 1) * PANEL] * hit(s, c * 10 + b)
        for g in range(4):
            wp_ref[g * 2 + s] = part[g * 24 : g * 24 + 24]
    pl.semaphore_wait(barrier, 23)

    def lp_copy(k):
        to = lax.rem(r + k, 16)
        return remote(
            lp_ref.at[to], lp_in.at[r], lps_sems.at[k], lpr_sems.at[k], {"row": to, "col": c}
        )

    def wp_copy(k):
        to = lax.rem(c + k, 8)
        return remote(
            wp_ref.at[to], wp_in.at[c], wps_sems.at[k], wpr_sems.at[k], {"row": r, "col": to}
        )

    def w_place(yh_of):
        return lambda pos, half: w_ref.at[(pos * 2 + yh_of) * 2 + core, pl.ds(half * 48, 48), :]

    def l_place(yl_of):
        return lambda pos, half: l_slot(pos * 2 + yl_of, half)

    w_rings = [
        Ring(w_place(yh), x, x_up, x_down, send_sems, recv_sems, 0),
        Ring(w_place(1 - yh), x, x_up, x_down, send_sems, recv_sems, 6),
    ]
    l_rings = [
        Ring(l_place(yl), z, z_up, z_down, send_sems, recv_sems, 12),
        Ring(l_place(1 - yl), z, z_up, z_down, send_sems, recv_sems, 18),
    ]
    pz = Ring(
        lambda pos, half: p_ref.at[core, y, x, pos, pl.ds(half * 24, 24), :],
        z, z_up, z_down, send_sems, recv_sems, 36,
    )
    px = Ring(
        lambda pos, half: p_ref.at[core, y, pos, pl.ds(half * 2, 2)],
        x, x_up, x_down, send_sems, recv_sems, 42,
    )
    spots = [x, px.pos(-1), px.pos(1), px.pos(2)]

    def w_own(half):
        return own_right.at[pl.ds(half * 48, 48), :]

    def l_own(half):
        return left_ref.at[pl.ds(half * 96, 96), :]

    swaps = []

    def swap(src, dst, key, target):
        copy = remote(src, dst, send_sems.at[key], recv_sems.at[key], target)
        copy.start()
        swaps.append(copy)

    def to_other(pos, yh_of, key):
        slot = w_ref.at[(pos * 2 + yh_of) * 2 + core]
        swap(slot, slot, key, other)

    def arrived(ref, key):
        remote(ref, ref, send_sems.at[key], recv_sems.at[key], other).wait_recv()

    def from_other(pos, yh_of, key):
        arrived(w_ref.at[(pos * 2 + yh_of) * 2 + 1 - core], key)

    def flow_w0():
        ring = w_rings[0]
        ring.start(0, w_own)
        yield
        ring.start(1, w_own)
        yield
        swap(own_right, w_ref.at[r], 28, other)
        ring.forward()
        yield
        ring.finish_near()
        to_other(ring.pos(-1), yh, 30)
        to_other(ring.pos(1), yh, 31)
        yield
        ring.finish_far()
        to_other(ring.pos(2), yh, 32)
        yield

    def flow_wy():
        for half in range(2):
            swap(w_own(half), w_place(yh)(x, half), 24 + half, far)
            yield

    def follow(ring, place, me, key):
        for half in range(2):
            ref = place(me, half)
            arrived(ref, key + half)
            ring.send(ref, me, half, half, ring.ahead)
            ring.send(ref, me, half, 2 + half, ring.behind)
            yield

    def flow_w1():
        ring = w_rings[1]
        yield from follow(ring, w_place(1 - yh), x, 24)
        to_other(x, 1 - yh, 29)
        ring.forward()
        yield
        ring.finish_near()
        to_other(ring.pos(-1), 1 - yh, 33)
        to_other(ring.pos(1), 1 - yh, 34)
        yield
        ring.finish_far()
        to_other(ring.pos(2), 1 - yh, 35)
        yield

    def flow_l0():
        ring = l_rings[0]
        ring.start(0, l_own)
        yield
        ring.start(1, l_own)
        yield
        ring.forward()
        yield

    def flow_ly():
        for half in range(2):
            swap(l_own(half), l_place(yl)(z, half), 26 + half, near)
            yield

    def flow_l1():
        ring = l_rings[1]
        yield from follow(ring, l_place(1 - yl), z, 26)
        ring.forward()
        yield

    def turn(pos):
        at_k = pl.ds(pl.multiple_of(pos * 384, 384), 384)

        @pl.loop(0, 5)
        def _(m):
            at_m = pl.ds(pl.multiple_of(m * PANEL, PANEL), PANEL)
            hi, lo = split(lt[at_k, at_m].T)
            lh[at_m, at_k] = hi
            ll[at_m, at_k] = lo

    def flow_t():
        put_l.wait()
        for ring in l_rings:
            ring.finish_near()
        for step in (0, -1, 1):
            turn(l_rings[0].pos(step))
        yield
        for ring in l_rings:
            ring.finish_far()
        turn(l_rings[0].pos(2))
        yield

    def flow_p():
        for k in range(1, 16):
            lp_copy(k).start()
        for k in range(1, 8):
            wp_copy(k).start()
        yield
        total_l = lp_ref[r]
        for k in range(1, 16):
            lp_copy(k).wait_recv()
        for k in range(1, 16):
            total_l = total_l + lp_in[lax.rem(r + 16 - k, 16)]
        total_w = wp_ref[c]
        for k in range(1, 8):
            wp_copy(k).wait_recv()
        for k in range(1, 8):
            total_w = total_w + wp_in[lax.rem(c + 8 - k, 8)]
        piece[pl.ds(0, 24), :] = total_l
        piece[pl.ds(24, 24), :] = total_w
        own_p = pltpu.make_async_copy(piece, p_ref.at[core, y, x, z], local_sems.at[2])
        own_p.start()
        for half in range(2):
            pz.start(half, lambda h: piece.at[pl.ds(h * 24, 24), :])
        yield
        pz.forward()
        yield
        def slot(y_of, i):
            return p_ref.at[core, y_of, spots[i]]

        def go(i):
            swap(slot(y, i), slot(y, i), 55 + 3 * i, near)
            swap(slot(y, i), slot(y, i), 56 + 3 * i, across)

        def onward(i):
            ref = slot(yh * 2 + 1 - yl, i)
            arrived(ref, 55 + 3 * i)
            swap(ref, ref, 57 + 3 * i, across)

        def share(i):
            arrived(slot(lax.rem(y + 3 + 2 * yl, 4), i), 56 + 3 * i)
            arrived(slot(lax.rem(y + 2, 4), i), 57 + 3 * i)
            whole = p_ref.at[core, pl.ds(0, 4), spots[i]]
            swap(whole, whole, 67 + i, other)

        own_p.wait()
        pz.finish_near()
        pz.finish_far()
        for half in range(2):
            px.start(half)
        go(0)
        yield
        px.forward()
        yield
        px.finish_near()
        go(1)
        go(2)
        onward(0)
        yield
        px.finish_far()
        go(3)
        onward(1)
        onward(2)
        yield
        share(0)
        onward(3)
        yield
        share(1)
        share(2)
        yield
        share(3)
        yield
        for i in range(4):
            arrived(p_ref.at[1 - core, pl.ds(0, 4), spots[i]], 67 + i)
        place_panels()
        yield

    def place_panels():
        @pl.loop(0, 32)
        def _(i):
            x_of, yh_of, z_of = i // 8, lax.rem(i // 4, 2), lax.rem(i, 4)
            for core_of in range(2):
                for yl_of in range(2):
                    block = p_ref[core_of, yh_of * 2 + yl_of, x_of, z_of]
                    at_l = pl.multiple_of((z_of * 2 + yl_of) * 192 + (x_of * 2 + yh_of) * 24, 24)
                    at_w = pl.multiple_of(
                        ((x_of * 2 + yh_of) * 2 + core_of) * 96 + z_of * 24, 24
                    )
                    lkt[pl.ds(at_l, 24), pl.ds(core_of * PANEL, PANEL)] = block[:24]
                    wk[pl.ds(at_w, 24), pl.ds(yl_of * PANEL, PANEL)] = block[24:]

    first, second = pl.ds(0, PANEL), pl.ds(PANEL, PANEL)

    def flow_chain():
        mids[...] = jnp.zeros_like(mids)

        @pl.loop(0, 6)
        def _(k):
            at_k = pl.ds(pl.multiple_of(k * PANEL, PANEL), PANEL)
            mids[...] += COUPLING * dot3(split(lkt[at_k, :].T), split(wk[at_k, :]))

        def screened(block, s):
            places = lax.broadcasted_iota(jnp.int32, (80, PANEL), 0)
            chosen = jnp.where(places == index_ref[:, s : s + 1], screen_ref[...], 0.0)
            return block + unit() * jnp.sum(chosen, axis=0, keepdims=True)

        inv1 = split(newton_inverse(screened(mids[first, first], 0)))
        x12 = split(mids[first, second])
        b1 = split(dot3(split(mids[second, first]), inv1))
        inv2 = split(newton_inverse(screened(mids[second, second] - dot3(b1, x12), 1)))
        yield
        for half in (first, second):
            cc[:, half] = COUPLING * dot3((lh[...], ll[...]), split(wk[:, half]))

        @pl.loop(0, 5)
        def _(m):
            at_m = pl.ds(pl.multiple_of(m * PANEL, PANEL), PANEL)
            mask1 = 1.0 - hit(0, r * 5 + m)
            mask2 = mask1 * (1.0 - hit(1, r * 5 + m))
            low1 = dot3(split(cc[at_m, first]), inv1) * mask1
            low2 = cc[at_m, second] - dot3(split(low1), x12)
            low2 = dot3(split(low2), inv2) * mask2
            lower[at_m, first] = low1
            lower[at_m, second] = low2
            pair = split(low2)
            eh[at_m, second], el[at_m, second] = pair
            eh[at_m, first], el[at_m, first] = split(low1 - dot3(pair, b1))

        put_lower.start()

        @pl.loop(0, 6)
        def _(k):
            at_k = pl.ds(pl.multiple_of(k * PANEL, PANEL), PANEL)
            panel = split(lkt[at_k, :])
            now = lh[:, at_k].astype(F32) + ll[:, at_k].astype(F32)
            now = now - dot3((eh[...], el[...]), panel, ((1,), (1,)))
            lh[:, at_k], ll[:, at_k] = split(now)
            for put in put_left(k):
                put.start()

        yield

    def put_left(k):
        at_k = pl.ds(pl.multiple_of(k * PANEL, PANEL), PANEL)
        return (
            pltpu.make_async_copy(lh.at[:, at_k], high_ref.at[:, at_k], left_sems.at[0, k]),
            pltpu.make_async_copy(ll.at[:, at_k], low_ref.at[:, at_k], left_sems.at[1, k]),
        )

    put_lower = pltpu.make_async_copy(lower, lower_ref, local_sems.at[4])

    makers = {
        "w0": flow_w0, "wy": flow_wy, "w1": flow_w1, "l0": flow_l0, "ly": flow_ly,
        "l1": flow_l1, "p": flow_p, "t": flow_t, "chain": flow_chain,
    }
    flows = {}
    for name in SCHEDULE:
        if name not in flows:
            flows[name] = makers[name]()
        next(flows[name])
    for flow in flows.values():
        for _ in flow:
            pass

    ring = w_rings[0]
    from_other(x, yh, 28)
    from_other(x, 1 - yh, 29)
    from_other(ring.pos(-1), yh, 30)
    from_other(ring.pos(1), yh, 31)
    from_other(ring.pos(2), yh, 32)
    from_other(ring.pos(-1), 1 - yh, 33)
    from_other(ring.pos(1), 1 - yh, 34)
    from_other(ring.pos(2), 1 - yh, 35)
    put_w.wait()
    put_lower.wait()
    for k in range(6):
        for put in put_left(k):
            put.wait()
    for k in range(1, 16):
        lp_copy(k).wait_send()
    for k in range(1, 8):
        wp_copy(k).wait_send()
    for ring in w_rings + l_rings + [pz, px]:
        ring.drain()
    for copy in swaps:
        copy.wait_send()


def gather(left_t, right, weight, index, screen):
    any_spec = pl.BlockSpec(memory_space=pl.ANY)
    vmem_spec = pl.BlockSpec(memory_space=pltpu.VMEM)
    dma = pltpu.SemaphoreType.DMA
    return pl.pallas_call(
        gather_kernel,
        out_shape=(
            jax.ShapeDtypeStruct((16, 96, 2560), F32),
            jax.ShapeDtypeStruct((1280, 1536), BF),
            jax.ShapeDtypeStruct((1280, 1536), BF),
            jax.ShapeDtypeStruct((1280, 512), F32),
        ),
        in_specs=[any_spec, any_spec, vmem_spec, vmem_spec, vmem_spec],
        out_specs=(any_spec, any_spec, any_spec, any_spec),
        scratch_shapes=[
            pltpu.VMEM((1536, 1280), F32),
            pltpu.VMEM((2, 4, 4, 4, 48, PANEL), F32),
            pltpu.VMEM((1536, 512), F32),
            pltpu.VMEM((1536, 512), F32),
            pltpu.VMEM((1280, 1536), BF),
            pltpu.VMEM((1280, 1536), BF),
            pltpu.VMEM((1280, 512), F32),
            pltpu.VMEM((1280, 512), F32),
            pltpu.VMEM((1280, 512), BF),
            pltpu.VMEM((1280, 512), BF),
            pltpu.VMEM((512, 512), F32),
            pltpu.VMEM((16, 24, PANEL), F32),
            pltpu.VMEM((8, 24, PANEL), F32),
            pltpu.VMEM((16, 24, PANEL), F32),
            pltpu.VMEM((8, 24, PANEL), F32),
            pltpu.VMEM((48, PANEL), F32),
            pltpu.VMEM((192, 1280), F32),
            pltpu.VMEM((96, 2560), F32),
            dma((71,)),
            dma((71,)),
            dma((16,)),
            dma((16,)),
            dma((8,)),
            dma((8,)),
            dma((6,)),
            dma((2, 6)),
        ],
        compiler_params=pltpu.CompilerParams(
            collective_id=0, has_side_effects=True, vmem_limit_bytes=58 << 20
        ),
        name="exchange",
    )(left_t, right, weight, index, screen)


def product_kernel(index_ref, lh_ref, ll_ref, w_ref, lower_ref, screen_ref, o_ref):
    n = pl.program_id(0)
    w = split(w_ref[...])
    o_ref[...] = COUPLING * dot3((lh_ref[...], ll_ref[...]), w)
    row0 = lax.axis_index("row") * 5
    block = lax.axis_index("col") * 10 + n
    rel = block - row0

    @pl.when((rel >= 0) & (rel < 5))
    def _():
        at = pl.ds(pl.multiple_of(rel * PANEL, PANEL), PANEL)
        o_ref[at, :] += unit() * screen_ref[pl.ds(block, 1), :]

    for s in range(2):

        @pl.when(block == index_ref[s])
        def _():
            for m in range(5):
                hit = row0 + m == index_ref[0]
                if s == 1:
                    hit = hit | (row0 + m == index_ref[1])

                @pl.when(jnp.logical_not(hit))
                def _():
                    at = pl.ds(m * PANEL, PANEL)
                    o_ref[at, :] = lower_ref[at, s * PANEL : (s + 1) * PANEL]


def product(index, lh, ll, w, lower, screen):
    once = dict(pipeline_mode=pl.Buffered(1))
    return pl.pallas_call(
        product_kernel,
        out_shape=jax.ShapeDtypeStruct((1280, 2560), F32),
        grid_spec=pltpu.PrefetchScalarGridSpec(
            num_scalar_prefetch=1,
            grid=(10,),
            in_specs=[
                pl.BlockSpec((1280, 1536), lambda n, s: (0, 0), **once),
                pl.BlockSpec((1280, 1536), lambda n, s: (0, 0), **once),
                pl.BlockSpec((1536, PANEL), lambda n, s: (0, n)),
                pl.BlockSpec((1280, 512), lambda n, s: (0, 0), **once),
                pl.BlockSpec((80, PANEL), lambda n, s: (0, 0), **once),
            ],
            out_specs=pl.BlockSpec((1280, PANEL), lambda n, s: (0, n)),
        ),
        compiler_params=pltpu.CompilerParams(vmem_limit_bytes=56 << 20),
        name="product",
    )(index, lh, ll, w, lower, screen)


def shards(left_pairs, right_pairs, pair_weight, screen, panel_index):
    screen = screen.reshape(80, PANEL)
    w_all, lh, ll, lower = gather(
        left_pairs.T,
        right_pairs,
        pair_weight.reshape(1, 96),
        panel_index.reshape(1, SECTIONS),
        screen,
    )
    return product(panel_index, lh, ll, w_all.reshape(1536, 2560), lower, screen)


def solution(mesh):
    return jax.shard_map(
        shards,
        mesh=mesh,
        in_specs=(P("row", "col"), P("row", "col"), P("row"), P(), P()),
        out_specs=P("row", "col"),
        check_vma=False,
    )
```
